32 devices in a mesh: dp: 4 (over y, core), expert: 8 (over z, x).
Axes of the slice: x: 2, y: 2, z: 4, core: 2. Of those that a mesh axis runs over, the one named last changes fastest.
Arguments:
- tokens: bfloat16 [2048, 7168], P('expert', 'dp'), may hold values from -6 to 6
- cotangent: bfloat16 [2048, 7168], P('expert', 'dp'), may hold values from -1.796875 to 1.796875
- expert_ids: int32 [2048, 8], P('expert'), may hold values from 0 to 255, as said below
- route_probs: bfloat16 [2048, 8], P('expert'), may hold values from 0.099609375 to 1
- w_up: bfloat16 [8, 7168, 1024], P('expert', 'dp'), may hold values from -0.0625 to 0.0625
- w_down: bfloat16 [8, 1024, 7168], P('expert', None, 'dp'), may hold values from -0.1875 to 0.1875
Outputs:
- grad_tokens: bfloat16 [2048, 7168], P('expert', 'dp')
- grad_probs: bfloat16 [2048, 8], P('expert')
- grad_up: bfloat16 [8, 7168, 1024], P('expert', 'dp')
- grad_down: bfloat16 [8, 1024, 7168], P('expert', None, 'dp')
The draws below stay inside these ranges and needn't reach their ends.
Inputs may be any that keep to these rules, and one draw needn't show every extreme that they name: `expert_ids`: A token names each id at most once. Within one block of 256 tokens each id below 8 is named by at most 8 tokens; one such id is named by exactly 8 tokens in every block, and in most blocks another one too; loads of the ids below 8 are strongly uneven.
All inputs are finite; a program needn't handle non-finite values.
Results may differ from the reference program's by a relative error of at most 0.008.
Values may be sent and summed in bfloat16 or wider, within the bound.
No kernel may reach another device: no remote copies, remote signals or barrier semaphores. Data moves between devices by JAX's collectives and lax.ppermute only.
A program may use at most 64 MiB of HBM per device.

```python
import jax
import jax.numpy as jnp
from jax import lax

D = 7168
FF = 1024
ROUTED = 256
TOP = 8
CAP = 8
TOK_DEV = 256
EXPERTS = 8
SLABS = 4
TOKENS = 2048


def draw_expert_ids(key, part):
    block_count = TOKENS // TOK_DEV
    hot_key, rest_key = jax.random.split(key)
    hot_global = jax.random.randint(hot_key, (), 0, EXPERTS)
    block_keys = jax.random.split(rest_key, block_count)

    def one_block(block_key):
        sub_keys = jax.random.split(block_key, 6)
        first = jax.random.randint(sub_keys[0], (EXPERTS,), 0, CAP + 1)
        second = jax.random.randint(sub_keys[1], (EXPERTS,), 0, CAP + 1)
        counts = first * second // CAP
        hot_local = jax.random.randint(sub_keys[2], (), 0, EXPERTS)
        expert_index = jnp.arange(EXPERTS, dtype=jnp.int32)
        counts = jnp.where((expert_index == hot_global) | (expert_index == hot_local), CAP, counts)
        starts = jnp.cumsum(counts) - counts
        positions = jnp.arange(TOP * TOK_DEV, dtype=jnp.int32)
        inside = (positions[:, None] >= starts[None, :]) & (positions[:, None] < (starts + counts)[None, :])
        owner_id = jnp.sum(jnp.where(inside, expert_index[None, :], 0), axis=1)
        is_live = jnp.any(inside, axis=1)
        offset_draw = jax.random.randint(sub_keys[3], (TOK_DEV,), 0, ROUTED - EXPERTS)
        layer_of = positions // TOK_DEV
        token_of = positions % TOK_DEV
        outside = EXPERTS + (offset_draw[token_of] + layer_of) % (ROUTED - EXPERTS)
        id_grid = jnp.where(is_live, owner_id, outside).reshape(TOP, TOK_DEV).T
        token_order = jax.random.permutation(sub_keys[4], TOK_DEV)
        id_grid = id_grid[token_order]
        scores = jax.random.randint(sub_keys[5], (TOK_DEV, TOP), 0, 1024) * TOP + jnp.arange(TOP, dtype=jnp.int32)[None, :]
        column_order = jnp.argsort(scores, axis=1)
        return jnp.take_along_axis(id_grid, column_order, axis=1)
    return jax.vmap(one_block)(block_keys).reshape(TOKENS, TOP).astype(jnp.int32)


def level_of(stream_key, dims, shards, smallest, largest):
    loudness, own = 1.0, jax.random.fold_in(stream_key, 6)
    for axis_at, parts in shards:
        heights = jnp.exp(jax.random.uniform(jax.random.fold_in(own, axis_at), (parts,), jnp.float32, smallest / len(shards), largest / len(shards)))
        loudness = loudness * jnp.repeat(heights, dims[axis_at] // parts).reshape([-1 if axis == axis_at else 1 for axis in range(len(dims))])
    return loudness


def centred(rng, dims, scale, limit, shards=(), kind=jnp.bfloat16):
    values = jax.random.normal(rng, dims, jnp.float32) * scale
    if len(shards) > 0:
        values = level_of(rng, dims, shards, -0.22, 0.18) * values
    return jnp.clip(values, min=-limit, max=limit).astype(kind)


def setup_inputs(seed: int = 0) -> dict:
    streams_of = jax.random.split(jax.random.key(seed), 7)
    return {
        "tokens": centred(streams_of[0], (TOKENS, D), 1.0, 6.0, ((0, 8), (1, 4))),
        "cotangent": centred(streams_of[1], (TOKENS, D), 0.3, 1.796875, ((0, 8), (1, 4))),
        "expert_ids": draw_expert_ids(jax.random.fold_in(streams_of[6], 71), 0),
        "route_probs": jnp.clip(0.099609375 + 0.9003906 * jax.random.uniform(streams_of[3], (TOKENS, TOP), jnp.float32) ** level_of(streams_of[3], (TOKENS, TOP), ((0, 8),), -0.2, 0.2), 0.099609375, 1.0).astype(jnp.bfloat16),
        "w_up": centred(streams_of[4], (EXPERTS, D, FF), D ** -0.5, 0.0625, ((0, 8), (1, 4))),
        "w_down": centred(streams_of[5], (EXPERTS, FF, D), FF ** -0.5, 0.1875, ((0, 8), (2, 4))),
    }


def sum_blocks(partials):
    return jnp.sum(partials, axis=0)


def reference(tokens, cotangent, expert_ids, route_probs, w_up, w_down):
    row_total = EXPERTS * CAP
    slab_width = D // SLABS
    numbers = jnp.arange(EXPERTS, dtype=jnp.int32)
    chosen = (expert_ids[:, :, None] == numbers[None, None, :]).astype(jnp.int32)
    per_token = jnp.sum(chosen, axis=1).reshape(EXPERTS, TOK_DEV, EXPERTS)
    before = (jnp.cumsum(per_token, axis=1) - per_token).reshape(TOKENS, EXPERTS)
    order_rank = jnp.sum(chosen * before[:, None, :], axis=2)
    block_of = (jnp.arange(TOKENS, dtype=jnp.int32) // TOK_DEV)[:, None]
    target = jnp.where(expert_ids < EXPERTS, expert_ids * row_total + block_of * CAP + order_rank, EXPERTS * row_total)
    slot_ids = jnp.arange(TOKENS * TOP, dtype=jnp.int32)
    table = jnp.full((EXPERTS * row_total,), TOKENS * TOP, jnp.int32)
    table = table.at[target.reshape(-1).astype(jnp.int32)].set(slot_ids, mode="drop").reshape(EXPERTS, row_total)
    token_pad = jnp.concatenate([tokens, jnp.zeros((1, D), tokens.dtype)], axis=0)
    cot_pad = jnp.concatenate([cotangent, jnp.zeros((1, D), cotangent.dtype)], axis=0)
    prob_pad = jnp.concatenate([route_probs.reshape(-1), jnp.zeros((1,), route_probs.dtype)], axis=0)

    def expert_step(carry, inputs):
        grad_acc, prob_acc = carry
        slot_rows, up_weight, down_weight = inputs
        token_of = jnp.minimum(slot_rows // TOP, TOKENS).astype(jnp.int32)
        rows_x = token_pad[token_of]
        rows_dy = cot_pad[token_of]
        gate_rows = prob_pad[slot_rows].astype(jnp.float32)
        hidden = sum_blocks(jnp.einsum("rjd,jdf->jrf", rows_x.reshape(row_total, SLABS, slab_width).astype(jnp.float32), up_weight.reshape(SLABS, slab_width, FF).astype(jnp.float32)))
        query = sum_blocks(jnp.einsum("rjd,fjd->jrf", rows_dy.reshape(row_total, SLABS, slab_width).astype(jnp.float32), down_weight.reshape(FF, SLABS, slab_width).astype(jnp.float32)))
        sigma_h = jax.nn.sigmoid(hidden)
        act_rows = (hidden * sigma_h).astype(jnp.bfloat16)
        score_rows = jnp.sum(act_rows.astype(jnp.float32) * query, axis=1).astype(jnp.bfloat16)
        hidden_grad = (gate_rows[:, None] * query * sigma_h * (1.0 + hidden * (1.0 - sigma_h))).astype(jnp.bfloat16)
        scaled = (gate_rows[:, None] * rows_dy.astype(jnp.float32)).astype(jnp.bfloat16)
        row_grad = jnp.dot(hidden_grad, up_weight.T, preferred_element_type=jnp.float32).astype(jnp.bfloat16)
        grad_acc = grad_acc.at[token_of].add(row_grad.astype(jnp.float32))
        prob_acc = prob_acc.at[slot_rows].add(score_rows.astype(jnp.float32))
        grad_upper = jnp.dot(rows_x.T, hidden_grad, preferred_element_type=jnp.float32).astype(jnp.bfloat16)
        grad_lower = jnp.dot(act_rows.T, scaled, preferred_element_type=jnp.float32).astype(jnp.bfloat16)
        return (grad_acc, prob_acc), (grad_upper, grad_lower)

    start = (jnp.zeros((TOKENS + 1, D), jnp.float32), jnp.zeros((TOKENS * TOP + 1,), jnp.float32))
    (grad_acc, prob_acc), (grad_up, grad_down) = lax.scan(expert_step, start, (table, w_up, w_down))
    grad_tokens = grad_acc[:TOKENS].astype(jnp.bfloat16)
    grad_probs = prob_acc[:TOKENS * TOP].reshape(TOKENS, TOP).astype(jnp.bfloat16)
    return (grad_tokens, grad_probs, grad_up, grad_down)
```

```python
import jax
import jax.numpy as jnp
from jax import lax
from jax.sharding import PartitionSpec as P

CAP = 8
LANES = 128


def contract(left, right, left_dim, right_dim):
    return lax.dot_general(
        left, right, (((left_dim,), (right_dim,)), ((), ())), preferred_element_type=jnp.float32
    )


def swap(value, bit):
    count = lax.axis_size("dp")
    return lax.ppermute(value, "dp", [(i, i ^ bit) for i in range(count)])


def on_device(tokens, cotangent, expert_ids, route_probs, w_up, w_down):
    experts = lax.axis_size("expert")
    dp_count = lax.axis_size("dp")
    block_rows, feat_width = tokens.shape
    hidden_units = w_up.shape[2]
    slot_count = experts * CAP
    paired = dp_count > 1 and dp_count & (dp_count - 1) == 0
    slots = jnp.arange(slot_count, dtype=jnp.int32)
    hit = expert_ids[:, :, None] == (slots // CAP)[None, None, :]
    member = jnp.any(hit, axis=1).astype(jnp.bfloat16)
    gate_of = jnp.sum(jnp.where(hit, route_probs[:, :, None], 0), axis=1).astype(jnp.float32)
    times = jnp.arange(block_rows, dtype=jnp.int32)
    earlier = (times[:, None] > times[None, :]).astype(jnp.bfloat16)
    rank = contract(earlier, member, 1, 0)
    holder = jnp.where(rank == (slots % CAP).astype(jnp.float32)[None, :], member, 0)
    gates = jnp.sum(holder.astype(jnp.float32) * gate_of, axis=0)
    stacked = jnp.concatenate([tokens, cotangent], axis=1)
    outgoing = contract(holder, stacked, 0, 0).astype(jnp.bfloat16)
    gate_cols = jnp.broadcast_to(gates.astype(jnp.bfloat16)[:, None], (slot_count, LANES))
    send = jnp.concatenate([outgoing, gate_cols], axis=1).reshape(experts, CAP, -1)
    rows = lax.all_to_all(send, "expert", split_axis=0, concat_axis=0, tiled=True)
    rows = rows.reshape(slot_count, -1)
    rows_x = rows[:, :feat_width]
    rows_dy = rows[:, feat_width : 2 * feat_width]
    gate_rows = rows[:, 2 * feat_width : 2 * feat_width + 1].astype(jnp.float32)
    up_weight = w_up[0]
    down_weight = w_down[0]
    part = jnp.concatenate(
        [jnp.dot(rows_x, up_weight, preferred_element_type=jnp.float32), contract(rows_dy, down_weight, 1, 1)],
        axis=1,
    )
    if paired:
        half = slot_count // 2
        core = lax.axis_index("dp") & 1
        gives = lax.dynamic_slice_in_dim(part, (1 - core) * half, half, 0).astype(jnp.bfloat16)
        total = lax.dynamic_slice_in_dim(part, core * half, half, 0) + swap(gives, 1).astype(jnp.float32)
        bit = 2
        while bit < dp_count:
            rounded = lax.reduce_precision(total, 8, 7)
            total = rounded + swap(rounded.astype(jnp.bfloat16), bit).astype(jnp.float32)
            bit *= 2
        gate_part = lax.dynamic_slice_in_dim(gate_rows, core * half, half, 0)
    else:
        total = lax.psum(part, "dp")
        gate_part = gate_rows
    hidden = total[:, :hidden_units]
    query = total[:, hidden_units:]
    sigma_h = jax.nn.sigmoid(hidden)
    act = (hidden * sigma_h).astype(jnp.bfloat16)
    score = jnp.sum(act.astype(jnp.float32) * query, axis=1, keepdims=True).astype(jnp.bfloat16)
    hidden_grad = (gate_part * query * sigma_h * (1.0 + hidden * (1.0 - sigma_h))).astype(jnp.bfloat16)
    packed = jnp.concatenate(
        [act, hidden_grad, jnp.broadcast_to(score, (score.shape[0], LANES))], axis=1
    )
    if paired:
        other = swap(packed, 1)
        low = jnp.where(core == 0, packed, other)
        high = jnp.where(core == 0, other, packed)
        packed = jnp.concatenate([low, high], axis=0)
    act = packed[:, :hidden_units]
    hidden_grad = packed[:, hidden_units : 2 * hidden_units]
    scaled = (gate_rows * rows_dy.astype(jnp.float32)).astype(jnp.bfloat16)
    row_grad = contract(hidden_grad, up_weight, 1, 1).astype(jnp.bfloat16)
    back = jnp.concatenate([row_grad, packed[:, 2 * hidden_units :]], axis=1).reshape(experts, CAP, -1)
    back = lax.all_to_all(back, "expert", split_axis=0, concat_axis=0, tiled=True)
    back = back.reshape(slot_count, -1)
    grad_up = contract(rows_x, hidden_grad, 0, 0).astype(jnp.bfloat16)[None]
    grad_down = contract(act, scaled, 0, 0).astype(jnp.bfloat16)[None]
    grad_tokens = contract(holder, back[:, :feat_width], 1, 0).astype(jnp.bfloat16)
    own = (slots[:, None] // CAP == jnp.arange(experts, dtype=jnp.int32)[None, :])
    by_expert = contract(holder, jnp.where(own, back[:, feat_width : feat_width + 1], 0), 1, 0)
    picks = expert_ids[:, :, None] == jnp.arange(experts, dtype=jnp.int32)[None, None, :]
    grad_probs = jnp.sum(jnp.where(picks, by_expert[:, None, :], 0), axis=2).astype(jnp.bfloat16)
    return (grad_tokens, grad_probs, grad_up, grad_down)


def solution(mesh):
    in_specs = (
        P("expert", "dp"),
        P("expert", "dp"),
        P("expert", None),
        P("expert", None),
        P("expert", "dp", None),
        P("expert", None, "dp"),
    )
    out_specs = (
        P("expert", "dp"),
        P("expert", None),
        P("expert", "dp", None),
        P("expert", None, "dp"),
    )
    return jax.shard_map(
        on_device, mesh=mesh, in_specs=in_specs, out_specs=out_specs, check_vma=False
    )
```

```python
import jax
import jax.numpy as jnp
from jax import lax
from jax.experimental import pallas as pl
from jax.experimental.pallas import tpu as pltpu
from jax.sharding import PartitionSpec as P

CAP = 8
LANES = 128
VMEM = pl.BlockSpec(memory_space=pltpu.VMEM)
ANY = pl.BlockSpec(memory_space=pl.ANY)
HBM = pl.BlockSpec(memory_space=pltpu.HBM)


def contract(left, right, left_dim, right_dim):
    return lax.dot_general(
        left, right, (((left_dim,), (right_dim,)), ((), ())), preferred_element_type=jnp.float32
    )


def swap(value, bit):
    count = lax.axis_size("dp")
    return lax.ppermute(value, "dp", [(i, i ^ bit) for i in range(count)])


def padded(width):
    return -(-width // LANES) * LANES


def chunks(width, wanted):
    return [(at, min(at + wanted, width)) for at in range(0, width, wanted)]


def in_vmem(value):
    return pltpu.with_memory_space_constraint(value, pltpu.VMEM)


def in_hbm(value):
    return pltpu.with_memory_space_constraint(value, pltpu.HBM)


def params(mib):
    return pltpu.CompilerParams(vmem_limit_bytes=mib << 20)


def cost(flops, nbytes):
    return pl.CostEstimate(flops=flops, bytes_accessed=nbytes, transcendentals=0)


def route(ids, probs, tokens, cotangent, up_weight, down_weight, slot_count):
    names, block_rows = ids.shape
    width = tokens.shape[1]
    step = padded(width)
    parts = chunks(width, padded(-(-width // 2)))

    def kernel(
        ids_ref, probs_ref, tok_hbm, cot_hbm, up_hbm, down_hbm,
        send_ref, hold_ref, up_ref, down_ref,
        tok, cot, out, in_sems, out_sems, weight_sems,
    ):
        jobs = []
        for source, target, base in ((tok_hbm, tok, 0), (cot_hbm, cot, step)):
            for low, high in parts:
                n = len(jobs)
                copy = pltpu.make_async_copy(
                    source.at[:, low:high], target.at[:, low:high], in_sems.at[n]
                )
                copy.start()
                jobs.append((copy, target, base, low, high))
        loads = [
            pltpu.make_async_copy(up_hbm, up_ref, weight_sems.at[0]),
            pltpu.make_async_copy(down_hbm, down_ref, weight_sems.at[1]),
        ]
        for load in loads:
            load.start()
        slots = lax.broadcasted_iota(jnp.int32, (slot_count, block_rows), 0)
        shift = CAP.bit_length() - 1
        expert = lax.shift_right_logical(slots, shift)
        place = (slots & (CAP - 1)).astype(jnp.float32)
        member = jnp.zeros((slot_count, block_rows), jnp.float32)
        gate = jnp.zeros((slot_count, block_rows), jnp.float32)
        for k in range(names):
            named = ids_ref[k : k + 1, :] == expert
            member = jnp.where(named, 1.0, member)
            gate = jnp.where(named, probs_ref[k : k + 1, :].astype(jnp.float32), gate)
        before = lax.broadcasted_iota(jnp.int32, (block_rows, block_rows), 0)
        after = lax.broadcasted_iota(jnp.int32, (block_rows, block_rows), 1)
        earlier = jnp.where(before < after, 1.0, 0.0).astype(jnp.bfloat16)
        rank = contract(member.astype(jnp.bfloat16), earlier, 1, 0)
        held = jnp.where(rank == place, member, 0.0)
        gates = jnp.sum(held * gate, axis=1, keepdims=True)
        hold = held.astype(jnp.bfloat16)
        hold_ref[...] = hold
        out[:, 2 * step :] = jnp.broadcast_to(gates, (slot_count, LANES)).astype(jnp.bfloat16)
        outs = [pltpu.make_async_copy(
            out.at[:, 2 * step :], send_ref.at[:, 2 * step :], out_sems.at[len(jobs)]
        )]
        outs[0].start()
        for n, (copy, target, base, low, high) in enumerate(jobs):
            copy.wait()
            out[:, base + low : base + high] = contract(hold, target[:, low:high], 1, 0).astype(
                jnp.bfloat16
            )
            end = base + (step if high == width else high)
            push = pltpu.make_async_copy(
                out.at[:, base + low : end], send_ref.at[:, base + low : end], out_sems.at[n]
            )
            push.start()
            outs.append(push)
        for push in outs + loads:
            push.wait()

    count = 2 * len(parts)
    return pl.pallas_call(
        kernel,
        out_shape=(
            jax.ShapeDtypeStruct((slot_count, 2 * step + LANES), jnp.bfloat16),
            jax.ShapeDtypeStruct((slot_count, block_rows), jnp.bfloat16),
            pltpu.VMEM(up_weight.shape, jnp.bfloat16),
            pltpu.VMEM(down_weight.shape, jnp.bfloat16),
        ),
        in_specs=[VMEM, VMEM, HBM, HBM, HBM, HBM],
        out_specs=(ANY, VMEM, VMEM, VMEM),
        scratch_shapes=[
            pltpu.VMEM(tokens.shape, jnp.bfloat16),
            pltpu.VMEM(tokens.shape, jnp.bfloat16),
            pltpu.VMEM((slot_count, 2 * step + LANES), jnp.bfloat16),
            pltpu.SemaphoreType.DMA((count,)),
            pltpu.SemaphoreType.DMA((count + 1,)),
            pltpu.SemaphoreType.DMA((2,)),
        ],
        compiler_params=params(16),
        cost_estimate=cost(4 * slot_count * block_rows * width, 8 * block_rows * width),
        name="route",
    )(ids, probs, *map(in_hbm, (tokens, cotangent, up_weight, down_weight)))


def core_rows(half):
    core = lax.axis_index("dp") & 1
    return pl.multiple_of(core * half, half), pl.multiple_of((1 - core) * half, half)


def products(rows, up_weight, down_weight):
    slot_count = rows.shape[0]
    half = slot_count // 2
    width, units = up_weight.shape
    step = padded(width)

    def kernel(rows_ref, up_ref, down_ref, give_ref, keep_ref, whole):
        mine, other = core_rows(half)
        for low, high in chunks(units, 256):
            whole[:, low:high] = contract(rows_ref[:, :width], up_ref[:, low:high], 1, 0)
        for low, high in chunks(units, 256):
            whole[:, units + low : units + high] = contract(
                rows_ref[:, step : step + width], down_ref[low:high, :], 1, 1
            )
        give_ref[...] = whole[pl.ds(other, half), :].astype(jnp.bfloat16)
        keep_ref[...] = whole[pl.ds(mine, half), :]

    return pl.pallas_call(
        kernel,
        out_shape=(
            jax.ShapeDtypeStruct((half, 2 * units), jnp.bfloat16),
            jax.ShapeDtypeStruct((half, 2 * units), jnp.float32),
        ),
        in_specs=[VMEM, VMEM, VMEM],
        out_specs=(VMEM, VMEM),
        scratch_shapes=[pltpu.VMEM((slot_count, 2 * units), jnp.float32)],
        compiler_params=params(24),
        cost_estimate=cost(4 * slot_count * width * units, 4 * width * units),
        name="products",
    )(rows, in_vmem(up_weight), in_vmem(down_weight))


def activate(rows, own, other, units, gate_at):
    half = own.shape[0]

    def kernel(rows_ref, own_ref, other_ref, out_ref):
        mine, _ = core_rows(half)
        gate = rows_ref[pl.ds(mine, half), gate_at : gate_at + LANES].astype(jnp.float32)[:, :1]
        total = own_ref[...].astype(jnp.float32) + other_ref[...].astype(jnp.float32)
        hidden = total[:, :units]
        query = total[:, units:]
        sigma_h = jax.nn.sigmoid(hidden)
        act = (hidden * sigma_h).astype(jnp.bfloat16)
        score = jnp.sum(act.astype(jnp.float32) * query, axis=1, keepdims=True)
        grad = gate * query * sigma_h * (1.0 + hidden * (1.0 - sigma_h))
        out_ref[:, :units] = act
        out_ref[:, units : 2 * units] = grad.astype(jnp.bfloat16)
        out_ref[:, 2 * units :] = jnp.broadcast_to(score, (half, LANES)).astype(jnp.bfloat16)

    return pl.pallas_call(
        kernel,
        out_shape=jax.ShapeDtypeStruct((half, 2 * units + LANES), jnp.bfloat16),
        in_specs=[VMEM, VMEM, VMEM],
        out_specs=VMEM,
        compiler_params=params(16),
        cost_estimate=cost(20 * half * units, 12 * half * units),
        name="activate",
    )(rows, own, other)


def returned(own, other, up_weight):
    half = own.shape[0]
    width, units = up_weight.shape
    step = padded(width)

    def kernel(own_ref, other_ref, up_ref, send_ref, act_ref, grad_ref, whole):
        mine, theirs = core_rows(half)
        whole[pl.ds(mine, half), :] = own_ref[...]
        whole[pl.ds(theirs, half), :] = other_ref[...]
        grad = whole[:, units : 2 * units]
        for low, high in chunks(width, 256):
            send_ref[:, low:high] = contract(grad, up_ref[low:high, :], 1, 1).astype(jnp.bfloat16)
        send_ref[:, step:] = whole[:, 2 * units :]
        act_ref[...] = whole[:, :units]
        grad_ref[...] = grad

    return pl.pallas_call(
        kernel,
        out_shape=(
            jax.ShapeDtypeStruct((2 * half, step + LANES), jnp.bfloat16),
            jax.ShapeDtypeStruct((2 * half, units), jnp.bfloat16),
            jax.ShapeDtypeStruct((2 * half, units), jnp.bfloat16),
        ),
        in_specs=[VMEM, VMEM, VMEM],
        out_specs=(VMEM,) * 3,
        scratch_shapes=[pltpu.VMEM((2 * half, own.shape[1]), jnp.bfloat16)],
        compiler_params=params(16),
        cost_estimate=cost(4 * half * width * units, 2 * width * units),
        name="returned",
    )(own, other, in_vmem(up_weight))


def collect(ids, hold, back, width):
    names, block_rows = ids.shape
    slot_count = hold.shape[0]
    experts = slot_count // CAP
    step = padded(width)
    parts = chunks(width, padded(-(-width // 2)))

    def kernel(ids_ref, hold_ref, back_ref, tok_ref, prob_ref, buf, sems):
        pushes = []
        for n, (low, high) in enumerate(parts):
            buf[:, low:high] = contract(hold_ref[...], back_ref[:, low:high], 0, 0).astype(jnp.bfloat16)
            push = pltpu.make_async_copy(buf.at[:, low:high], tok_ref.at[:, low:high], sems.at[n])
            push.start()
            pushes.append(push)
        scores = hold_ref[...].astype(jnp.float32) * back_ref[:, step : step + 1].astype(jnp.float32)
        total = jnp.zeros((names, block_rows), jnp.float32)
        for e in range(experts):
            score = jnp.sum(scores[e * CAP : (e + 1) * CAP, :], axis=0, keepdims=True)
            total = jnp.where(ids_ref[...] == e, score, total)
        prob_ref[...] = total.astype(jnp.bfloat16)
        for push in pushes:
            push.wait()

    return pl.pallas_call(
        kernel,
        out_shape=(
            jax.ShapeDtypeStruct((block_rows, width), jnp.bfloat16),
            jax.ShapeDtypeStruct((names, block_rows), jnp.bfloat16),
        ),
        in_specs=[VMEM, VMEM, VMEM],
        out_specs=(ANY, VMEM),
        scratch_shapes=[
            pltpu.VMEM((block_rows, width), jnp.bfloat16),
            pltpu.SemaphoreType.DMA((len(parts),)),
        ],
        compiler_params=params(16),
        cost_estimate=cost(2 * slot_count * block_rows * width, 4 * block_rows * width),
        name="collect",
    )(ids, hold, back)


def exchange(rows, experts):
    rows = rows.reshape(experts, CAP, -1)
    rows = lax.all_to_all(rows, "expert", split_axis=0, concat_axis=0, tiled=True)
    return rows.reshape(experts * CAP, -1)


def on_device(tokens, cotangent, expert_ids, route_probs, w_up, w_down):
    experts = lax.axis_size("expert")
    dp_count = lax.axis_size("dp")
    width = tokens.shape[1]
    step = padded(width)
    units = w_up.shape[2]
    slot_count = experts * CAP
    ids = expert_ids.T
    send, hold, up_weight, down_weight = route(
        ids, route_probs.T, tokens, cotangent, w_up[0], w_down[0], slot_count
    )
    rows = exchange(send, experts)
    gate_rows = rows[:, 2 * step : 2 * step + 1].astype(jnp.float32)
    if dp_count > 1 and dp_count & (dp_count - 1) == 0:
        gives, keeps = products(rows, up_weight, down_weight)
        own = (keeps + swap(gives, 1).astype(jnp.float32)).astype(jnp.bfloat16)
        other = jnp.zeros_like(own)
        bit = 2
        while bit < dp_count:
            if bit > 2:
                own = (own.astype(jnp.float32) + other.astype(jnp.float32)).astype(jnp.bfloat16)
            other = swap(own, bit)
            bit *= 2
        packed = activate(rows, own, other, units, 2 * step)
        back, act, hidden_grad = returned(packed, swap(packed, 1), up_weight)
    else:
        hidden = contract(rows[:, :width], up_weight, 1, 0)
        query = contract(rows[:, step : step + width], down_weight, 1, 1)
        hidden, query = lax.psum((hidden, query), "dp")
        sigma_h = jax.nn.sigmoid(hidden)
        act = (hidden * sigma_h).astype(jnp.bfloat16)
        score = jnp.sum(act.astype(jnp.float32) * query, axis=1, keepdims=True).astype(jnp.bfloat16)
        hidden_grad = gate_rows * query * sigma_h * (1.0 + hidden * (1.0 - sigma_h))
        hidden_grad = hidden_grad.astype(jnp.bfloat16)
        pad = jnp.zeros((slot_count, step - width), jnp.bfloat16)
        row_grad = contract(hidden_grad, up_weight, 1, 1).astype(jnp.bfloat16)
        back = jnp.concatenate([row_grad, pad, jnp.broadcast_to(score, (slot_count, LANES))], axis=1)
    back = exchange(back, experts)
    scaled = (gate_rows * rows[:, step : step + width].astype(jnp.float32)).astype(jnp.bfloat16)
    grad_up = contract(rows[:, :width], hidden_grad, 0, 0).astype(jnp.bfloat16)[None]
    grad_down = contract(act, scaled, 0, 0).astype(jnp.bfloat16)[None]
    grad_tokens, grad_probs = collect(ids, hold, back, width)
    return (grad_tokens, grad_probs.T, grad_up, grad_down)


def solution(mesh):
    in_specs = (
        P("expert", "dp"),
        P("expert", "dp"),
        P("expert", None),
        P("expert", None),
        P("expert", "dp", None),
        P("expert", None, "dp"),
    )
    out_specs = (
        P("expert", "dp"),
        P("expert", None),
        P("expert", "dp", None),
        P("expert", None, "dp"),
    )
    return jax.shard_map(
        on_device, mesh=mesh, in_specs=in_specs, out_specs=out_specs, check_vma=False
    )
```

```python
import jax
import jax.numpy as jnp
from jax import lax
from jax.experimental import pallas as pl
from jax.experimental.pallas import tpu as pltpu
from jax.sharding import PartitionSpec as P

CAP = 8
LANES = 128
VMEM = pl.BlockSpec(memory_space=pltpu.VMEM)
ANY = pl.BlockSpec(memory_space=pl.ANY)
HBM = pl.BlockSpec(memory_space=pltpu.HBM)


def contract(left, right, left_dim, right_dim):
    return lax.dot_general(
        left, right, (((left_dim,), (right_dim,)), ((), ())), preferred_element_type=jnp.float32
    )


def swap(value, bit):
    count = lax.axis_size("dp")
    return lax.ppermute(value, "dp", [(i, i ^ bit) for i in range(count)])


def padded(width):
    return -(-width // LANES) * LANES


def chunks(width, wanted):
    return [(at, min(at + wanted, width)) for at in range(0, width, wanted)]


def in_vmem(value):
    return pltpu.with_memory_space_constraint(value, pltpu.VMEM)


def in_hbm(value):
    return pltpu.with_memory_space_constraint(value, pltpu.HBM)


def params(mib):
    return pltpu.CompilerParams(vmem_limit_bytes=mib << 20)


def cost(flops, nbytes):
    return pl.CostEstimate(flops=flops, bytes_accessed=nbytes, transcendentals=0)


def route(ids, probs, tokens, cotangent, up_weight, slot_count):
    names, block_rows = ids.shape
    width = tokens.shape[1]
    step = padded(width)
    parts = chunks(width, padded(-(-width // 2)))

    def kernel(
        ids_hbm, probs_hbm, tok_hbm, cot_hbm, up_hbm,
        send_ref, hold_ref, up_ref,
        ids_ref, probs_ref, tok, cot, out, name_sems, in_sems, out_sems, weight_sems,
    ):
        small = [
            pltpu.make_async_copy(ids_hbm, ids_ref, name_sems.at[0]),
            pltpu.make_async_copy(probs_hbm, probs_ref, name_sems.at[1]),
        ]
        for copy in small:
            copy.start()
        jobs = []
        for source, target, base in ((tok_hbm, tok, 0), (cot_hbm, cot, step)):
            for low, high in parts:
                n = len(jobs)
                copy = pltpu.make_async_copy(
                    source.at[:, low:high], target.at[:, low:high], in_sems.at[n]
                )
                copy.start()
                jobs.append((copy, target, base, low, high))
        loads = []
        for n, (low, high) in enumerate(chunks(width, 448)):
            loads.append(
                pltpu.make_async_copy(up_hbm.at[low:high], up_ref.at[low:high], weight_sems.at[n])
            )
            loads[-1].start()
        slots = lax.broadcasted_iota(jnp.int32, (slot_count, block_rows), 0)
        expert = lax.shift_right_logical(slots, CAP.bit_length() - 1)
        place = (slots & (CAP - 1)).astype(jnp.float32)
        before = lax.broadcasted_iota(jnp.int32, (block_rows, block_rows), 0)
        after = lax.broadcasted_iota(jnp.int32, (block_rows, block_rows), 1)
        earlier = jnp.where(before < after, 1.0, 0.0).astype(jnp.bfloat16)
        member = jnp.zeros((slot_count, block_rows), jnp.float32)
        gate = jnp.zeros((slot_count, block_rows), jnp.float32)
        for copy in small:
            copy.wait()
        for k in range(names):
            named = ids_ref[k : k + 1, :] == expert
            member = jnp.where(named, 1.0, member)
            gate = jnp.where(named, probs_ref[k : k + 1, :].astype(jnp.float32), gate)
        rank = contract(member.astype(jnp.bfloat16), earlier, 1, 0)
        held = jnp.where(rank == place, member, 0.0)
        gates = jnp.sum(held * gate, axis=1, keepdims=True)
        hold = held.astype(jnp.bfloat16)
        hold_ref[...] = hold
        outs = []
        for n, (copy, target, base, low, high) in enumerate(jobs):
            copy.wait()
            rows = contract(hold, target[:, low:high], 1, 0)
            if base:
                rows = rows * gates
            out[:, base + low : base + high] = rows.astype(jnp.bfloat16)
            end = base + (step if high == width else high)
            push = pltpu.make_async_copy(
                out.at[:, base + low : end], send_ref.at[:, base + low : end], out_sems.at[n]
            )
            push.start()
            outs.append(push)
        for push in outs + loads:
            push.wait()

    count = 2 * len(parts)
    return pl.pallas_call(
        kernel,
        out_shape=(
            jax.ShapeDtypeStruct((slot_count, 2 * step), jnp.bfloat16),
            jax.ShapeDtypeStruct((slot_count, block_rows), jnp.bfloat16),
            pltpu.VMEM(up_weight.shape, jnp.bfloat16),
        ),
        in_specs=[HBM] * 5,
        out_specs=(ANY, VMEM, VMEM),
        scratch_shapes=[
            pltpu.VMEM(ids.shape, ids.dtype),
            pltpu.VMEM(probs.shape, probs.dtype),
            pltpu.VMEM(tokens.shape, jnp.bfloat16),
            pltpu.VMEM(tokens.shape, jnp.bfloat16),
            pltpu.VMEM((slot_count, 2 * step), jnp.bfloat16),
            pltpu.SemaphoreType.DMA((2,)),
            pltpu.SemaphoreType.DMA((count,)),
            pltpu.SemaphoreType.DMA((count,)),
            pltpu.SemaphoreType.DMA((len(chunks(width, 448)),)),
        ],
        compiler_params=params(16),
        cost_estimate=cost(4 * slot_count * block_rows * width, 8 * block_rows * width),
        name="route",
    )(*map(in_hbm, (ids, probs, tokens, cotangent, up_weight)))


def core_rows(half):
    core = lax.axis_index("dp") & 1
    return pl.multiple_of(core * half, half), pl.multiple_of((1 - core) * half, half)


def products(rows, up_weight, down_weight):
    slot_count = rows.shape[0]
    half = slot_count // 2
    width, units = up_weight.shape
    step = padded(width)

    parts = chunks(units, 256)

    def kernel(rows_ref, up_ref, down_hbm, give_ref, keep_ref, whole, down_ref, sems):
        loads = []
        for n, (low, high) in enumerate(parts):
            loads.append(
                pltpu.make_async_copy(down_hbm.at[low:high], down_ref.at[low:high], sems.at[n])
            )
            loads[-1].start()
        mine, other = core_rows(half)
        for low, high in parts:
            whole[:, low:high] = contract(rows_ref[:, :width], up_ref[:, low:high], 1, 0)
        for (low, high), load in zip(parts, loads):
            load.wait()
            whole[:, units + low : units + high] = contract(
                rows_ref[:, step : step + width], down_ref[low:high, :], 1, 1
            )
        give_ref[...] = whole[pl.ds(other, half), :].astype(jnp.bfloat16)
        keep_ref[...] = whole[pl.ds(mine, half), :]

    return pl.pallas_call(
        kernel,
        out_shape=(
            jax.ShapeDtypeStruct((half, 2 * units), jnp.bfloat16),
            jax.ShapeDtypeStruct((half, 2 * units), jnp.float32),
        ),
        in_specs=[VMEM, VMEM, HBM],
        out_specs=(VMEM, VMEM),
        scratch_shapes=[
            pltpu.VMEM((slot_count, 2 * units), jnp.float32),
            pltpu.VMEM(down_weight.shape, jnp.bfloat16),
            pltpu.SemaphoreType.DMA((len(parts),)),
        ],
        compiler_params=params(24),
        cost_estimate=cost(4 * slot_count * width * units, 4 * width * units),
        name="products",
    )(rows, in_vmem(up_weight), in_hbm(down_weight))


def activate(own, other, units):
    half = own.shape[0]

    def kernel(own_ref, other_ref, out_ref):
        total = own_ref[...].astype(jnp.float32) + other_ref[...].astype(jnp.float32)
        hidden = total[:, :units]
        query = total[:, units:]
        sigma_h = jax.nn.sigmoid(hidden)
        act = (hidden * sigma_h).astype(jnp.bfloat16)
        score = jnp.sum(act.astype(jnp.float32) * query, axis=1, keepdims=True)
        grad = query * sigma_h * (1.0 + hidden * (1.0 - sigma_h))
        out_ref[:, :units] = act
        out_ref[:, units : 2 * units] = grad.astype(jnp.bfloat16)
        out_ref[:, 2 * units :] = jnp.broadcast_to(score, (half, LANES)).astype(jnp.bfloat16)

    return pl.pallas_call(
        kernel,
        out_shape=jax.ShapeDtypeStruct((half, 2 * units + LANES), jnp.bfloat16),
        in_specs=[VMEM, VMEM],
        out_specs=VMEM,
        compiler_params=params(16),
        cost_estimate=cost(20 * half * units, 12 * half * units),
        name="activate",
    )(own, other)


def returned(own, other, up_weight):
    half = own.shape[0]
    width, units = up_weight.shape
    step = padded(width)
    parts = chunks(width, 256)

    def kernel(own_ref, other_ref, up_ref, send_ref, act_ref, grad_ref, out, sems):
        for at, source in zip(core_rows(half), (own_ref, other_ref)):
            act_ref[pl.ds(at, half), :] = source[:, :units]
            grad_ref[pl.ds(at, half), :] = source[:, units : 2 * units]
            out[pl.ds(at, half), step:] = source[:, 2 * units :]
        pushes = []
        for n, (low, high) in enumerate(parts):
            out[:, low:high] = contract(grad_ref[...], up_ref[low:high, :], 1, 1).astype(jnp.bfloat16)
            end = step + LANES if high == width else high
            push = pltpu.make_async_copy(out.at[:, low:end], send_ref.at[:, low:end], sems.at[n])
            push.start()
            pushes.append(push)
        for push in pushes:
            push.wait()

    return pl.pallas_call(
        kernel,
        out_shape=(
            jax.ShapeDtypeStruct((2 * half, step + LANES), jnp.bfloat16),
            jax.ShapeDtypeStruct((2 * half, units), jnp.bfloat16),
            jax.ShapeDtypeStruct((2 * half, units), jnp.bfloat16),
        ),
        in_specs=[VMEM, VMEM, VMEM],
        out_specs=(ANY, VMEM, VMEM),
        scratch_shapes=[
            pltpu.VMEM((2 * half, step + LANES), jnp.bfloat16),
            pltpu.SemaphoreType.DMA((len(parts),)),
        ],
        compiler_params=params(16),
        cost_estimate=cost(4 * half * width * units, 2 * width * units),
        name="returned",
    )(own, other, in_vmem(up_weight))


def collect(ids, probs, hold, back, width):
    names, block_rows = ids.shape
    slot_count = hold.shape[0]
    experts = slot_count // CAP
    step = padded(width)
    parts = chunks(width, 256)

    def kernel(ids_ref, probs_ref, hold_ref, back_ref, tok_ref, prob_ref, buf, sems):
        pushes = []
        for n, (low, high) in enumerate(parts):
            buf[:, low:high] = contract(hold_ref[...], back_ref[:, low:high], 0, 0).astype(jnp.bfloat16)
            push = pltpu.make_async_copy(buf.at[:, low:high], tok_ref.at[:, low:high], sems.at[n])
            push.start()
            pushes.append(push)
        scores = hold_ref[...].astype(jnp.float32) * back_ref[:, step : step + 1].astype(jnp.float32)
        total = jnp.zeros((names, block_rows), jnp.float32)
        for e in range(experts):
            score = jnp.sum(scores[e * CAP : (e + 1) * CAP, :], axis=0, keepdims=True)
            total = jnp.where(ids_ref[...] == e, score, total)
        prob_ref[...] = (total / probs_ref[...].astype(jnp.float32)).astype(jnp.bfloat16)
        for push in pushes:
            push.wait()

    return pl.pallas_call(
        kernel,
        out_shape=(
            jax.ShapeDtypeStruct((block_rows, width), jnp.bfloat16),
            jax.ShapeDtypeStruct((names, block_rows), jnp.bfloat16),
        ),
        in_specs=[VMEM] * 4,
        out_specs=(ANY, VMEM),
        scratch_shapes=[
            pltpu.VMEM((block_rows, width), jnp.bfloat16),
            pltpu.SemaphoreType.DMA((len(parts),)),
        ],
        compiler_params=params(16),
        cost_estimate=cost(2 * slot_count * block_rows * width, 4 * block_rows * width),
        name="collect",
    )(ids, probs, hold, back)


def exchange(rows, experts):
    rows = rows.reshape(experts, CAP, -1)
    rows = lax.all_to_all(rows, "expert", split_axis=0, concat_axis=0, tiled=True)
    return rows.reshape(experts * CAP, -1)


def on_device(tokens, cotangent, expert_ids, route_probs, w_up, w_down):
    experts = lax.axis_size("expert")
    dp_count = lax.axis_size("dp")
    width = tokens.shape[1]
    step = padded(width)
    units = w_up.shape[2]
    slot_count = experts * CAP
    ids = expert_ids.T
    probs = route_probs.T
    down_weight = w_down[0]
    send, hold, up_weight = route(ids, probs, tokens, cotangent, w_up[0], slot_count)
    rows = exchange(send, experts)
    if dp_count > 1 and dp_count & (dp_count - 1) == 0:
        gives, keeps = products(rows, up_weight, down_weight)
        own = (keeps + swap(gives, 1).astype(jnp.float32)).astype(jnp.bfloat16)
        other = jnp.zeros_like(own)
        bit = 2
        while bit < dp_count:
            if bit > 2:
                own = (own.astype(jnp.float32) + other.astype(jnp.float32)).astype(jnp.bfloat16)
            other = swap(own, bit)
            bit *= 2
        packed = activate(own, other, units)
        back, act, hidden_grad = returned(packed, swap(packed, 1), up_weight)
    else:
        hidden = contract(rows[:, :width], up_weight, 1, 0)
        query = contract(rows[:, step : step + width], down_weight, 1, 1)
        hidden, query = lax.psum((hidden, query), "dp")
        sigma_h = jax.nn.sigmoid(hidden)
        act = (hidden * sigma_h).astype(jnp.bfloat16)
        score = jnp.sum(act.astype(jnp.float32) * query, axis=1, keepdims=True).astype(jnp.bfloat16)
        hidden_grad = (query * sigma_h * (1.0 + hidden * (1.0 - sigma_h))).astype(jnp.bfloat16)
        pad = jnp.zeros((slot_count, step - width), jnp.bfloat16)
        row_grad = contract(hidden_grad, up_weight, 1, 1).astype(jnp.bfloat16)
        back = jnp.concatenate([row_grad, pad, jnp.broadcast_to(score, (slot_count, LANES))], axis=1)
    back = exchange(back, experts)
    grad_up = contract(rows[:, :width], hidden_grad, 0, 0).astype(jnp.bfloat16)[None]
    grad_down = contract(act, rows[:, step : step + width], 0, 0).astype(jnp.bfloat16)[None]
    grad_tokens, grad_probs = collect(ids, probs, hold, back, width)
    return (grad_tokens, grad_probs.T, grad_up, grad_down)


def solution(mesh):
    in_specs = (
        P("expert", "dp"),
        P("expert", "dp"),
        P("expert", None),
        P("expert", None),
        P("expert", "dp", None),
        P("expert", None, "dp"),
    )
    out_specs = (
        P("expert", "dp"),
        P("expert", None),
        P("expert", "dp", None),
        P("expert", None, "dp"),
    )
    return jax.shard_map(
        on_device, mesh=mesh, in_specs=in_specs, out_specs=out_specs, check_vma=False
    )
```

```python
import jax
import jax.numpy as jnp
from jax import lax
from jax.experimental import pallas as pl
from jax.experimental.pallas import tpu as pltpu
from jax.sharding import PartitionSpec as P

CAP = 8
LANES = 128
VMEM = pl.BlockSpec(memory_space=pltpu.VMEM)
ANY = pl.BlockSpec(memory_space=pl.ANY)
HBM = pl.BlockSpec(memory_space=pltpu.HBM)


def contract(left, right, left_dim, right_dim):
    return lax.dot_general(
        left, right, (((left_dim,), (right_dim,)), ((), ())), preferred_element_type=jnp.float32
    )


def swap(value, bit):
    count = lax.axis_size("dp")
    return lax.ppermute(value, "dp", [(i, i ^ bit) for i in range(count)])


def padded(width):
    return -(-width // LANES) * LANES


def chunks(width, wanted):
    return [(at, min(at + wanted, width)) for at in range(0, width, wanted)]


def in_vmem(value):
    return pltpu.with_memory_space_constraint(value, pltpu.VMEM)


def in_hbm(value):
    return pltpu.with_memory_space_constraint(value, pltpu.HBM)


def params(mib):
    return pltpu.CompilerParams(vmem_limit_bytes=mib << 20)


def cost(flops, nbytes):
    return pl.CostEstimate(flops=flops, bytes_accessed=nbytes, transcendentals=0)


def route(ids, probs, tokens, cotangent, weights, slot_count):
    names, block_rows = ids.shape
    width = tokens.shape[1]
    step = padded(width)

    def kernel(ids_hbm, probs_hbm, tok_hbm, cot_hbm, *refs):
        send_ref, hold_ref, ids_ref, probs_ref, tok, cot, sems = refs[len(weights) :]
        copies = [
            pltpu.make_async_copy(source, target, sems.at[n])
            for n, (source, target) in enumerate(
                ((ids_hbm, ids_ref), (probs_hbm, probs_ref), (tok_hbm, tok), (cot_hbm, cot))
            )
        ]
        for copy in copies:
            copy.start()
        slots = lax.broadcasted_iota(jnp.int32, (slot_count, block_rows), 0)
        expert = lax.shift_right_logical(slots, CAP.bit_length() - 1)
        place = (slots & (CAP - 1)).astype(jnp.float32)
        before = lax.broadcasted_iota(jnp.int32, (block_rows, block_rows), 0)
        after = lax.broadcasted_iota(jnp.int32, (block_rows, block_rows), 1)
        earlier = jnp.where(before < after, 1.0, 0.0).astype(jnp.bfloat16)
        member = jnp.zeros((slot_count, block_rows), jnp.float32)
        gate = jnp.zeros((slot_count, block_rows), jnp.float32)
        copies[0].wait()
        copies[1].wait()
        for k in range(names):
            named = ids_ref[k : k + 1, :] == expert
            member = jnp.where(named, 1.0, member)
            gate = jnp.where(named, probs_ref[k : k + 1, :].astype(jnp.float32), gate)
        rank = contract(member.astype(jnp.bfloat16), earlier, 1, 0)
        held = jnp.where(rank == place, member, 0.0)
        gates = jnp.sum(held * gate, axis=1, keepdims=True)
        hold = held.astype(jnp.bfloat16)
        hold_ref[...] = hold
        copies[2].wait()
        for low, high in chunks(width, 256):
            send_ref[:, low:high] = contract(hold, tok[:, low:high], 1, 0).astype(jnp.bfloat16)
        copies[3].wait()
        for low, high in chunks(width, 256):
            rows = contract(hold, cot[:, low:high], 1, 0) * gates
            send_ref[:, step + low : step + high] = rows.astype(jnp.bfloat16)

    return pl.pallas_call(
        kernel,
        out_shape=(
            pltpu.VMEM((slot_count, 2 * step), jnp.bfloat16),
            pltpu.VMEM((slot_count, block_rows), jnp.bfloat16),
        ),
        in_specs=[HBM] * (4 + len(weights)),
        out_specs=(VMEM, VMEM),
        scratch_shapes=[
            pltpu.VMEM(ids.shape, ids.dtype),
            pltpu.VMEM(probs.shape, probs.dtype),
            pltpu.VMEM(tokens.shape, jnp.bfloat16),
            pltpu.VMEM(tokens.shape, jnp.bfloat16),
            pltpu.SemaphoreType.DMA((4,)),
        ],
        compiler_params=params(8),
        cost_estimate=cost(4 * slot_count * block_rows * width, 8 * block_rows * width),
        name="route",
    )(*map(in_hbm, (ids, probs, tokens, cotangent, *weights)))


def core_rows(half):
    core = lax.axis_index("dp") & 1
    return pl.multiple_of(core * half, half), pl.multiple_of((1 - core) * half, half)


def split(hidden, query):
    rows, units = hidden.shape
    half = rows // 2

    def kernel(hidden_ref, query_ref, give_ref, keep_ref):
        mine, other = core_rows(half)
        for at, source in ((0, hidden_ref), (units, query_ref)):
            give_ref[:, at : at + units] = source[pl.ds(other, half), :].astype(jnp.bfloat16)
            keep_ref[:, at : at + units] = source[pl.ds(mine, half), :]

    return pl.pallas_call(
        kernel,
        out_shape=(
            jax.ShapeDtypeStruct((half, 2 * units), jnp.bfloat16),
            jax.ShapeDtypeStruct((half, 2 * units), jnp.float32),
        ),
        in_specs=[VMEM, VMEM],
        out_specs=(VMEM, VMEM),
        compiler_params=params(8),
        cost_estimate=cost(0, 12 * half * units),
        name="split",
    )(hidden, query)


def activate(own, other, units):
    half = own.shape[0]

    def kernel(own_ref, other_ref, out_ref):
        total = own_ref[...].astype(jnp.float32) + other_ref[...].astype(jnp.float32)
        hidden = total[:, :units]
        query = total[:, units:]
        sigma_h = jax.nn.sigmoid(hidden)
        act = (hidden * sigma_h).astype(jnp.bfloat16)
        score = jnp.sum(act.astype(jnp.float32) * query, axis=1, keepdims=True)
        grad = query * sigma_h * (1.0 + hidden * (1.0 - sigma_h))
        out_ref[:, :units] = act
        out_ref[:, units : 2 * units] = grad.astype(jnp.bfloat16)
        out_ref[:, 2 * units :] = jnp.broadcast_to(score, (half, LANES)).astype(jnp.bfloat16)

    return pl.pallas_call(
        kernel,
        out_shape=jax.ShapeDtypeStruct((half, 2 * units + LANES), jnp.bfloat16),
        in_specs=[VMEM, VMEM],
        out_specs=VMEM,
        compiler_params=params(16),
        cost_estimate=cost(20 * half * units, 12 * half * units),
        name="activate",
    )(own, other)


def returned(own, other, up_weight):
    half = own.shape[0]
    width, units = up_weight.shape
    step = padded(width)

    def kernel(own_ref, other_ref, up_ref, send_ref, act_ref, grad_ref):
        for at, source in zip(core_rows(half), (own_ref, other_ref)):
            act_ref[pl.ds(at, half), :] = source[:, :units]
            grad_ref[pl.ds(at, half), :] = source[:, units : 2 * units]
            send_ref[pl.ds(at, half), step:] = source[:, 2 * units :]
        for low, high in chunks(width, 256):
            send_ref[:, low:high] = contract(grad_ref[...], up_ref[low:high, :], 1, 1).astype(
                jnp.bfloat16
            )

    return pl.pallas_call(
        kernel,
        out_shape=(
            pltpu.VMEM((2 * half, step + LANES), jnp.bfloat16),
            pltpu.VMEM((2 * half, units), jnp.bfloat16),
            pltpu.VMEM((2 * half, units), jnp.bfloat16),
        ),
        in_specs=[VMEM, VMEM, VMEM],
        out_specs=(VMEM, VMEM, VMEM),
        compiler_params=params(8),
        cost_estimate=cost(4 * half * width * units, 2 * width * units),
        name="returned",
    )(own, other, in_vmem(up_weight))


def collect(ids, probs, hold, back, width):
    names, block_rows = ids.shape
    slot_count = hold.shape[0]
    experts = slot_count // CAP
    step = padded(width)
    parts = chunks(width, 256)

    def kernel(ids_ref, probs_ref, hold_ref, back_ref, tok_ref, prob_ref, buf, sems):
        pushes = []
        for n, (low, high) in enumerate(parts):
            buf[:, low:high] = contract(hold_ref[...], back_ref[:, low:high], 0, 0).astype(jnp.bfloat16)
            push = pltpu.make_async_copy(buf.at[:, low:high], tok_ref.at[:, low:high], sems.at[n])
            push.start()
            pushes.append(push)
        scores = hold_ref[...].astype(jnp.float32) * back_ref[:, step : step + 1].astype(jnp.float32)
        total = jnp.zeros((names, block_rows), jnp.float32)
        for e in range(experts):
            score = jnp.sum(scores[e * CAP : (e + 1) * CAP, :], axis=0, keepdims=True)
            total = jnp.where(ids_ref[...] == e, score, total)
        prob_ref[...] = (total / probs_ref[...].astype(jnp.float32)).astype(jnp.bfloat16)
        for push in pushes:
            push.wait()

    return pl.pallas_call(
        kernel,
        out_shape=(
            jax.ShapeDtypeStruct((block_rows, width), jnp.bfloat16),
            jax.ShapeDtypeStruct((names, block_rows), jnp.bfloat16),
        ),
        in_specs=[VMEM] * 4,
        out_specs=(ANY, VMEM),
        scratch_shapes=[
            pltpu.VMEM((block_rows, width), jnp.bfloat16),
            pltpu.SemaphoreType.DMA((len(parts),)),
        ],
        compiler_params=params(16),
        cost_estimate=cost(2 * slot_count * block_rows * width, 4 * block_rows * width),
        name="collect",
    )(ids, probs, hold, back)


def exchange(rows, experts):
    rows = rows.reshape(experts, CAP, -1)
    rows = lax.all_to_all(rows, "expert", split_axis=0, concat_axis=0, tiled=True)
    return rows.reshape(experts * CAP, -1)


def on_device(tokens, cotangent, expert_ids, route_probs, w_up, w_down):
    experts = lax.axis_size("expert")
    dp_count = lax.axis_size("dp")
    width = tokens.shape[1]
    step = padded(width)
    units = w_up.shape[2]
    slot_count = experts * CAP
    ids = expert_ids.T
    probs = route_probs.T
    up_weight = w_up[0]
    down_weight = w_down[0]
    send, hold = route(ids, probs, tokens, cotangent, (up_weight, down_weight), slot_count)
    rows = exchange(send, experts)
    if dp_count > 1 and dp_count & (dp_count - 1) == 0:
        hidden = contract(rows[:, :width], up_weight, 1, 0)
        hidden, ahead = lax.optimization_barrier((hidden, rows))
        gives, keeps = split(hidden, contract(ahead[:, step : step + width], down_weight, 1, 1))
        own = (keeps + swap(gives, 1).astype(jnp.float32)).astype(jnp.bfloat16)
        other = jnp.zeros_like(own)
        bit = 2
        while bit < dp_count:
            if bit > 2:
                own = (own.astype(jnp.float32) + other.astype(jnp.float32)).astype(jnp.bfloat16)
            other = swap(own, bit)
            bit *= 2
        packed = activate(own, other, units)
        back, act, hidden_grad = returned(packed, swap(packed, 1), up_weight)
    else:
        hidden = contract(rows[:, :width], up_weight, 1, 0)
        query = contract(rows[:, step : step + width], down_weight, 1, 1)
        hidden, query = lax.psum((hidden, query), "dp")
        sigma_h = jax.nn.sigmoid(hidden)
        act = (hidden * sigma_h).astype(jnp.bfloat16)
        score = jnp.sum(act.astype(jnp.float32) * query, axis=1, keepdims=True).astype(jnp.bfloat16)
        hidden_grad = (query * sigma_h * (1.0 + hidden * (1.0 - sigma_h))).astype(jnp.bfloat16)
        pad = jnp.zeros((slot_count, step - width), jnp.bfloat16)
        row_grad = contract(hidden_grad, up_weight, 1, 1).astype(jnp.bfloat16)
        back = jnp.concatenate([row_grad, pad, jnp.broadcast_to(score, (slot_count, LANES))], axis=1)
    back = exchange(back, experts)
    grad_up = contract(rows[:, :width], hidden_grad, 0, 0).astype(jnp.bfloat16)[None]
    grad_down = contract(act, rows[:, step : step + width], 0, 0).astype(jnp.bfloat16)[None]
    grad_tokens, grad_probs = collect(ids, probs, hold, back, width)
    return (grad_tokens, grad_probs.T, grad_up, grad_down)


def solution(mesh):
    in_specs = (
        P("expert", "dp"),
        P("expert", "dp"),
        P("expert", None),
        P("expert", None),
        P("expert", "dp", None),
        P("expert", None, "dp"),
    )
    out_specs = (
        P("expert", "dp"),
        P("expert", None),
        P("expert", "dp", None),
        P("expert", None, "dp"),
    )
    return jax.shard_map(
        on_device, mesh=mesh, in_specs=in_specs, out_specs=out_specs, check_vma=False
    )
```

```python
import jax
import jax.numpy as jnp
from jax import lax
from jax.experimental import pallas as pl
from jax.experimental.pallas import tpu as pltpu
from jax.sharding import PartitionSpec as P

CAP = 8
LANES = 128
VMEM = pl.BlockSpec(memory_space=pltpu.VMEM)
ANY = pl.BlockSpec(memory_space=pl.ANY)
HBM = pl.BlockSpec(memory_space=pltpu.HBM)


def contract(left, right, left_dim, right_dim):
    return lax.dot_general(
        left, right, (((left_dim,), (right_dim,)), ((), ())), preferred_element_type=jnp.float32
    )


def swap(value, bit):
    count = lax.axis_size("dp")
    return lax.ppermute(value, "dp", [(i, i ^ bit) for i in range(count)])


def padded(width):
    return -(-width // LANES) * LANES


def chunks(width, wanted):
    return [(at, min(at + wanted, width)) for at in range(0, width, wanted)]


def in_vmem(value):
    return pltpu.with_memory_space_constraint(value, pltpu.VMEM)


def in_hbm(value):
    return pltpu.with_memory_space_constraint(value, pltpu.HBM)


def params(mib):
    return pltpu.CompilerParams(vmem_limit_bytes=mib << 20)


def cost(flops, nbytes):
    return pl.CostEstimate(flops=flops, bytes_accessed=nbytes, transcendentals=0)


def route(ids, probs, tokens, cotangent, weights, slot_count):
    names, block_rows = ids.shape
    width = tokens.shape[1]
    step = padded(width)

    def kernel(ids_hbm, probs_hbm, tok_hbm, cot_hbm, *refs):
        send_ref, hold_ref, ids_ref, probs_ref, tok, cot, sems = refs[len(weights) :]
        copies = [
            pltpu.make_async_copy(source, target, sems.at[n])
            for n, (source, target) in enumerate(
                ((ids_hbm, ids_ref), (probs_hbm, probs_ref), (tok_hbm, tok), (cot_hbm, cot))
            )
        ]
        for copy in copies:
            copy.start()
        slots = lax.broadcasted_iota(jnp.int32, (slot_count, block_rows), 0)
        expert = lax.shift_right_logical(slots, CAP.bit_length() - 1)
        place = (slots & (CAP - 1)).astype(jnp.float32)
        before = lax.broadcasted_iota(jnp.int32, (block_rows, block_rows), 0)
        after = lax.broadcasted_iota(jnp.int32, (block_rows, block_rows), 1)
        earlier = jnp.where(before < after, 1.0, 0.0).astype(jnp.bfloat16)
        member = jnp.zeros((slot_count, block_rows), jnp.float32)
        gate = jnp.zeros((slot_count, block_rows), jnp.float32)
        copies[0].wait()
        copies[1].wait()
        for k in range(names):
            named = ids_ref[k : k + 1, :] == expert
            member = jnp.where(named, 1.0, member)
            gate = jnp.where(named, probs_ref[k : k + 1, :].astype(jnp.float32), gate)
        rank = contract(member.astype(jnp.bfloat16), earlier, 1, 0)
        held = jnp.where(rank == place, member, 0.0)
        gates = jnp.sum(held * gate, axis=1, keepdims=True)
        hold = held.astype(jnp.bfloat16)
        hold_ref[...] = hold
        copies[2].wait()
        for low, high in chunks(width, 256):
            send_ref[:, low:high] = contract(hold, tok[:, low:high], 1, 0).astype(jnp.bfloat16)
        copies[3].wait()
        for low, high in chunks(width, 256):
            rows = contract(hold, cot[:, low:high], 1, 0) * gates
            send_ref[:, step + low : step + high] = rows.astype(jnp.bfloat16)

    return pl.pallas_call(
        kernel,
        out_shape=(
            pltpu.VMEM((slot_count, 2 * step), jnp.bfloat16),
            pltpu.VMEM((slot_count, block_rows), jnp.bfloat16),
        ),
        in_specs=[HBM] * (4 + len(weights)),
        out_specs=(VMEM, VMEM),
        scratch_shapes=[
            pltpu.VMEM(ids.shape, ids.dtype),
            pltpu.VMEM(probs.shape, probs.dtype),
            pltpu.VMEM(tokens.shape, jnp.bfloat16),
            pltpu.VMEM(tokens.shape, jnp.bfloat16),
            pltpu.SemaphoreType.DMA((4,)),
        ],
        compiler_params=params(8),
        cost_estimate=cost(4 * slot_count * block_rows * width, 8 * block_rows * width),
        name="route",
    )(*map(in_hbm, (ids, probs, tokens, cotangent, *weights)))


def core_rows(half):
    core = lax.axis_index("dp") & 1
    return pl.multiple_of(core * half, half), pl.multiple_of((1 - core) * half, half)


def split(value):
    rows, units = value.shape
    half = rows // 2

    def kernel(value_ref, give_ref, keep_ref):
        mine, other = core_rows(half)
        give_ref[...] = value_ref[pl.ds(other, half), :].astype(jnp.bfloat16)
        keep_ref[...] = value_ref[pl.ds(mine, half), :]

    return pl.pallas_call(
        kernel,
        out_shape=(
            jax.ShapeDtypeStruct((half, units), jnp.bfloat16),
            jax.ShapeDtypeStruct((half, units), jnp.float32),
        ),
        in_specs=[VMEM],
        out_specs=(VMEM, VMEM),
        compiler_params=params(8),
        cost_estimate=cost(0, 10 * half * units),
        name="split",
    )(value)


def summed(give, keep):
    own = (keep + swap(give, 1).astype(jnp.float32)).astype(jnp.bfloat16)
    other = jnp.zeros_like(own)
    bit = 2
    while bit < lax.axis_size("dp"):
        if bit > 2:
            own = (own.astype(jnp.float32) + other.astype(jnp.float32)).astype(jnp.bfloat16)
        other = swap(own, bit)
        bit *= 2
    return own, other


def activate(*terms):
    half, units = terms[0].shape

    def kernel(hidden_own, hidden_other, query_own, query_other, out_ref):
        hidden = hidden_own[...].astype(jnp.float32) + hidden_other[...].astype(jnp.float32)
        query = query_own[...].astype(jnp.float32) + query_other[...].astype(jnp.float32)
        sigma_h = jax.nn.sigmoid(hidden)
        act = (hidden * sigma_h).astype(jnp.bfloat16)
        score = jnp.sum(act.astype(jnp.float32) * query, axis=1, keepdims=True)
        grad = query * sigma_h * (1.0 + hidden * (1.0 - sigma_h))
        out_ref[:, :units] = act
        out_ref[:, units : 2 * units] = grad.astype(jnp.bfloat16)
        out_ref[:, 2 * units :] = jnp.broadcast_to(score, (half, LANES)).astype(jnp.bfloat16)

    return pl.pallas_call(
        kernel,
        out_shape=jax.ShapeDtypeStruct((half, 2 * units + LANES), jnp.bfloat16),
        in_specs=[VMEM] * 4,
        out_specs=VMEM,
        compiler_params=params(16),
        cost_estimate=cost(20 * half * units, 12 * half * units),
        name="activate",
    )(*terms)


def returned(own, other, up_weight):
    half = own.shape[0]
    width, units = up_weight.shape
    step = padded(width)

    def kernel(own_ref, other_ref, up_ref, send_ref, act_ref, grad_ref):
        for at, source in zip(core_rows(half), (own_ref, other_ref)):
            act_ref[pl.ds(at, half), :] = source[:, :units]
            grad_ref[pl.ds(at, half), :] = source[:, units : 2 * units]
            send_ref[pl.ds(at, half), step:] = source[:, 2 * units :]
        for low, high in chunks(width, 256):
            send_ref[:, low:high] = contract(grad_ref[...], up_ref[low:high, :], 1, 1).astype(
                jnp.bfloat16
            )

    return pl.pallas_call(
        kernel,
        out_shape=(
            pltpu.VMEM((2 * half, step + LANES), jnp.bfloat16),
            pltpu.VMEM((2 * half, units), jnp.bfloat16),
            pltpu.VMEM((2 * half, units), jnp.bfloat16),
        ),
        in_specs=[VMEM, VMEM, VMEM],
        out_specs=(VMEM, VMEM, VMEM),
        compiler_params=params(8),
        cost_estimate=cost(4 * half * width * units, 2 * width * units),
        name="returned",
    )(own, other, in_vmem(up_weight))


def collect(ids, probs, hold, back, width):
    names, block_rows = ids.shape
    slot_count = hold.shape[0]
    experts = slot_count // CAP
    step = padded(width)
    parts = chunks(width, 256)

    def kernel(ids_ref, probs_ref, hold_ref, back_ref, tok_ref, prob_ref, buf, sems):
        pushes = []
        for n, (low, high) in enumerate(parts):
            buf[:, low:high] = contract(hold_ref[...], back_ref[:, low:high], 0, 0).astype(jnp.bfloat16)
            push = pltpu.make_async_copy(buf.at[:, low:high], tok_ref.at[:, low:high], sems.at[n])
            push.start()
            pushes.append(push)
        scores = hold_ref[...].astype(jnp.float32) * back_ref[:, step : step + 1].astype(jnp.float32)
        total = jnp.zeros((names, block_rows), jnp.float32)
        for e in range(experts):
            score = jnp.sum(scores[e * CAP : (e + 1) * CAP, :], axis=0, keepdims=True)
            total = jnp.where(ids_ref[...] == e, score, total)
        prob_ref[...] = (total / probs_ref[...].astype(jnp.float32)).astype(jnp.bfloat16)
        for push in pushes:
            push.wait()

    return pl.pallas_call(
        kernel,
        out_shape=(
            jax.ShapeDtypeStruct((block_rows, width), jnp.bfloat16),
            jax.ShapeDtypeStruct((names, block_rows), jnp.bfloat16),
        ),
        in_specs=[VMEM] * 4,
        out_specs=(ANY, VMEM),
        scratch_shapes=[
            pltpu.VMEM((block_rows, width), jnp.bfloat16),
            pltpu.SemaphoreType.DMA((len(parts),)),
        ],
        compiler_params=params(16),
        cost_estimate=cost(2 * slot_count * block_rows * width, 4 * block_rows * width),
        name="collect",
    )(ids, probs, hold, back)


def exchange(rows, experts):
    rows = rows.reshape(experts, CAP, -1)
    rows = lax.all_to_all(rows, "expert", split_axis=0, concat_axis=0, tiled=True)
    return rows.reshape(experts * CAP, -1)


def on_device(tokens, cotangent, expert_ids, route_probs, w_up, w_down):
    experts = lax.axis_size("expert")
    dp_count = lax.axis_size("dp")
    width = tokens.shape[1]
    step = padded(width)
    slot_count = experts * CAP
    ids = expert_ids.T
    probs = route_probs.T
    up_weight = w_up[0]
    down_weight = w_down[0]
    send, hold = route(ids, probs, tokens, cotangent, (up_weight, down_weight), slot_count)
    rows = exchange(send, experts)
    if dp_count > 1 and dp_count & (dp_count - 1) == 0:
        hidden = contract(rows[:, :width], up_weight, 1, 0)
        give, keep = split(hidden)
        give, ahead = lax.optimization_barrier((give, rows))
        query = contract(ahead[:, step : step + width], down_weight, 1, 1)
        hidden_terms = summed(give, keep)
        query_terms = summed(*split(query))
        packed = activate(*hidden_terms, *query_terms)
        back, act, hidden_grad = returned(packed, swap(packed, 1), up_weight)
    else:
        hidden = contract(rows[:, :width], up_weight, 1, 0)
        query = contract(rows[:, step : step + width], down_weight, 1, 1)
        hidden, query = lax.psum((hidden, query), "dp")
        sigma_h = jax.nn.sigmoid(hidden)
        act = (hidden * sigma_h).astype(jnp.bfloat16)
        score = jnp.sum(act.astype(jnp.float32) * query, axis=1, keepdims=True).astype(jnp.bfloat16)
        hidden_grad = (query * sigma_h * (1.0 + hidden * (1.0 - sigma_h))).astype(jnp.bfloat16)
        pad = jnp.zeros((slot_count, step - width), jnp.bfloat16)
        row_grad = contract(hidden_grad, up_weight, 1, 1).astype(jnp.bfloat16)
        back = jnp.concatenate([row_grad, pad, jnp.broadcast_to(score, (slot_count, LANES))], axis=1)
    back = exchange(back, experts)
    grad_up = contract(rows[:, :width], hidden_grad, 0, 0).astype(jnp.bfloat16)[None]
    grad_down = contract(act, rows[:, step : step + width], 0, 0).astype(jnp.bfloat16)[None]
    grad_tokens, grad_probs = collect(ids, probs, hold, back, width)
    return (grad_tokens, grad_probs.T, grad_up, grad_down)


def solution(mesh):
    in_specs = (
        P("expert", "dp"),
        P("expert", "dp"),
        P("expert", None),
        P("expert", None),
        P("expert", "dp", None),
        P("expert", None, "dp"),
    )
    out_specs = (
        P("expert", "dp"),
        P("expert", None),
        P("expert", "dp", None),
        P("expert", None, "dp"),
    )

    return jax.shard_map(on_device, mesh=mesh, in_specs=in_specs, out_specs=out_specs, check_vma=False)
```

```python
import jax
import jax.numpy as jnp
from jax import lax
from jax.experimental import pallas as pl
from jax.experimental.pallas import tpu as pltpu
from jax.sharding import PartitionSpec as P

CAP = 8
LANES = 128
VMEM = pl.BlockSpec(memory_space=pltpu.VMEM)
ANY = pl.BlockSpec(memory_space=pl.ANY)
HBM = pl.BlockSpec(memory_space=pltpu.HBM)


def contract(left, right, left_dim, right_dim):
    return lax.dot_general(
        left, right, (((left_dim,), (right_dim,)), ((), ())), preferred_element_type=jnp.float32
    )


def swap(value, bit):
    count = lax.axis_size("dp")
    return lax.ppermute(value, "dp", [(i, i ^ bit) for i in range(count)])


def padded(width):
    return -(-width // LANES) * LANES


def chunks(width, wanted):
    return [(at, min(at + wanted, width)) for at in range(0, width, wanted)]


def in_vmem(value):
    return pltpu.with_memory_space_constraint(value, pltpu.VMEM)


def in_hbm(value):
    return pltpu.with_memory_space_constraint(value, pltpu.HBM)


def params(mib):
    return pltpu.CompilerParams(vmem_limit_bytes=mib << 20)


def cost(flops, nbytes):
    return pl.CostEstimate(flops=flops, bytes_accessed=nbytes, transcendentals=0)


def reorder(rows, me):
    count = rows.shape[0]
    here = lax.broadcasted_iota(jnp.int32, (count, count), 0)
    there = lax.broadcasted_iota(jnp.int32, (count, count), 1)
    moves = jnp.where(here == (there ^ (me * CAP)), 1.0, 0.0).astype(jnp.bfloat16)
    return contract(moves, rows, 1, 0).astype(jnp.bfloat16)


def route(ids, probs, tokens, cotangent, weights, slot_count, direct):
    names, block_rows = ids.shape
    width = tokens.shape[1]
    step = padded(width)

    def kernel(ids_hbm, probs_hbm, tok_hbm, cot_hbm, *refs):
        *send_refs, hold_ref, ids_ref, probs_ref, tok, cot, sems = refs[len(weights) :]
        me = lax.axis_index("expert") if direct else 0

        def store(rows, low, high):
            each = slot_count // len(send_refs)
            for j, send_ref in enumerate(send_refs):
                send_ref[:, low:high] = rows[j * each : (j + 1) * each].astype(jnp.bfloat16)

        copies = [
            pltpu.make_async_copy(source, target, sems.at[n])
            for n, (source, target) in enumerate(
                ((ids_hbm, ids_ref), (probs_hbm, probs_ref), (tok_hbm, tok), (cot_hbm, cot))
            )
        ]
        for copy in copies:
            copy.start()
        slots = lax.broadcasted_iota(jnp.int32, (slot_count, block_rows), 0)
        expert = lax.shift_right_logical(slots, CAP.bit_length() - 1) ^ me
        place = (slots & (CAP - 1)).astype(jnp.float32)
        before = lax.broadcasted_iota(jnp.int32, (block_rows, block_rows), 0)
        after = lax.broadcasted_iota(jnp.int32, (block_rows, block_rows), 1)
        earlier = jnp.where(before < after, 1.0, 0.0).astype(jnp.bfloat16)
        member = jnp.zeros((slot_count, block_rows), jnp.float32)
        gate = jnp.zeros((slot_count, block_rows), jnp.float32)
        copies[0].wait()
        copies[1].wait()
        for k in range(names):
            named = ids_ref[k : k + 1, :] == expert
            member = jnp.where(named, 1.0, member)
            gate = jnp.where(named, probs_ref[k : k + 1, :].astype(jnp.float32), gate)
        rank = contract(member.astype(jnp.bfloat16), earlier, 1, 0)
        held = jnp.where(rank == place, member, 0.0)
        gates = jnp.sum(held * gate, axis=1, keepdims=True)
        hold = held.astype(jnp.bfloat16)
        hold_ref[...] = reorder(hold, me) if direct else hold
        copies[2].wait()
        for low, high in chunks(width, 256):
            store(contract(hold, tok[:, low:high], 1, 0), low, high)
        copies[3].wait()
        for low, high in chunks(width, 256):
            store(contract(hold, cot[:, low:high], 1, 0) * gates, step + low, step + high)

    pieces = slot_count // CAP if direct else 1
    *send, hold = pl.pallas_call(
        kernel,
        out_shape=(pltpu.VMEM((slot_count // pieces, 2 * step), jnp.bfloat16),) * pieces
        + (pltpu.VMEM((slot_count, block_rows), jnp.bfloat16),),
        in_specs=[HBM] * (4 + len(weights)),
        out_specs=(VMEM,) * (pieces + 1),
        scratch_shapes=[
            pltpu.VMEM(ids.shape, ids.dtype),
            pltpu.VMEM(probs.shape, probs.dtype),
            pltpu.VMEM(tokens.shape, jnp.bfloat16),
            pltpu.VMEM(tokens.shape, jnp.bfloat16),
            pltpu.SemaphoreType.DMA((4,)),
        ],
        compiler_params=params(8),
        cost_estimate=cost(4 * slot_count * block_rows * width, 8 * block_rows * width),
        name="route",
    )(*map(in_hbm, (ids, probs, tokens, cotangent, *weights)))
    return send, hold


def core_rows(half):
    core = lax.axis_index("dp") & 1
    return pl.multiple_of(core * half, half), pl.multiple_of((1 - core) * half, half)


def split(value):
    rows, units = value.shape
    half = rows // 2

    def kernel(value_ref, give_ref, keep_ref):
        mine, other = core_rows(half)
        give_ref[...] = value_ref[pl.ds(other, half), :].astype(jnp.bfloat16)
        keep_ref[...] = value_ref[pl.ds(mine, half), :]

    return pl.pallas_call(
        kernel,
        out_shape=(
            jax.ShapeDtypeStruct((half, units), jnp.bfloat16),
            jax.ShapeDtypeStruct((half, units), jnp.float32),
        ),
        in_specs=[VMEM],
        out_specs=(VMEM, VMEM),
        compiler_params=params(8),
        cost_estimate=cost(0, 10 * half * units),
        name="split",
    )(value)


def summed(give, keep):
    own = (keep + swap(give, 1).astype(jnp.float32)).astype(jnp.bfloat16)
    other = jnp.zeros_like(own)
    bit = 2
    while bit < lax.axis_size("dp"):
        if bit > 2:
            own = (own.astype(jnp.float32) + other.astype(jnp.float32)).astype(jnp.bfloat16)
        other = swap(own, bit)
        bit *= 2
    return own, other


def activate(*terms):
    half, units = terms[0].shape

    def kernel(hidden_own, hidden_other, query_own, query_other, out_ref):
        hidden = hidden_own[...].astype(jnp.float32) + hidden_other[...].astype(jnp.float32)
        query = query_own[...].astype(jnp.float32) + query_other[...].astype(jnp.float32)
        sigma_h = jax.nn.sigmoid(hidden)
        act = (hidden * sigma_h).astype(jnp.bfloat16)
        score = jnp.sum(act.astype(jnp.float32) * query, axis=1, keepdims=True)
        grad = query * sigma_h * (1.0 + hidden * (1.0 - sigma_h))
        out_ref[:, :units] = act
        out_ref[:, units : 2 * units] = grad.astype(jnp.bfloat16)
        out_ref[:, 2 * units :] = jnp.broadcast_to(score, (half, LANES)).astype(jnp.bfloat16)

    return pl.pallas_call(
        kernel,
        out_shape=jax.ShapeDtypeStruct((half, 2 * units + LANES), jnp.bfloat16),
        in_specs=[VMEM] * 4,
        out_specs=VMEM,
        compiler_params=params(16),
        cost_estimate=cost(20 * half * units, 12 * half * units),
        name="activate",
    )(*terms)


def returned(own, other, up_weight, direct):
    half = own.shape[0]
    width, units = up_weight.shape
    step = padded(width)

    def kernel(own_ref, other_ref, up_ref, send_ref, act_ref, grad_ref):
        for at, source in zip(core_rows(half), (own_ref, other_ref)):
            act_ref[pl.ds(at, half), :] = source[:, :units]
            grad_ref[pl.ds(at, half), :] = source[:, units : 2 * units]
            send_ref[pl.ds(at, half), step:] = source[:, 2 * units :]
        grad = grad_ref[...]
        if direct:
            me = lax.axis_index("expert")
            grad = reorder(grad, me)
            send_ref[:, step:] = reorder(send_ref[:, step:], me)
        for low, high in chunks(width, 256):
            send_ref[:, low:high] = contract(grad, up_ref[low:high, :], 1, 1).astype(
                jnp.bfloat16
            )

    return pl.pallas_call(
        kernel,
        out_shape=(
            pltpu.VMEM((2 * half, step + LANES), jnp.bfloat16),
            pltpu.VMEM((2 * half, units), jnp.bfloat16),
            pltpu.VMEM((2 * half, units), jnp.bfloat16),
        ),
        in_specs=[VMEM, VMEM, VMEM],
        out_specs=(VMEM, VMEM, VMEM),
        compiler_params=params(8),
        cost_estimate=cost(4 * half * width * units, 2 * width * units),
        name="returned",
    )(own, other, in_vmem(up_weight))


def collect(ids, probs, hold, back, width):
    names, block_rows = ids.shape
    slot_count = hold.shape[0]
    experts = slot_count // CAP
    step = padded(width)
    parts = chunks(width, 256)

    def kernel(ids_ref, probs_ref, hold_ref, back_ref, tok_ref, prob_ref, buf, sems):
        pushes = []
        for n, (low, high) in enumerate(parts):
            buf[:, low:high] = contract(hold_ref[...], back_ref[:, low:high], 0, 0).astype(jnp.bfloat16)
            push = pltpu.make_async_copy(buf.at[:, low:high], tok_ref.at[:, low:high], sems.at[n])
            push.start()
            pushes.append(push)
        scores = hold_ref[...].astype(jnp.float32) * back_ref[:, step : step + 1].astype(jnp.float32)
        total = jnp.zeros((names, block_rows), jnp.float32)
        for e in range(experts):
            score = jnp.sum(scores[e * CAP : (e + 1) * CAP, :], axis=0, keepdims=True)
            total = jnp.where(ids_ref[...] == e, score, total)
        prob_ref[...] = (total / probs_ref[...].astype(jnp.float32)).astype(jnp.bfloat16)
        for push in pushes:
            push.wait()

    return pl.pallas_call(
        kernel,
        out_shape=(
            jax.ShapeDtypeStruct((block_rows, width), jnp.bfloat16),
            jax.ShapeDtypeStruct((names, block_rows), jnp.bfloat16),
        ),
        in_specs=[VMEM] * 4,
        out_specs=(ANY, VMEM),
        scratch_shapes=[
            pltpu.VMEM((block_rows, width), jnp.bfloat16),
            pltpu.SemaphoreType.DMA((len(parts),)),
        ],
        compiler_params=params(16),
        cost_estimate=cost(2 * slot_count * block_rows * width, 4 * block_rows * width),
        name="collect",
    )(ids, probs, hold, back)


def dispatch(pieces):
    count = len(pieces)
    got = [pieces[0]]
    for j in range(1, count):
        got.append(lax.ppermute(pieces[j], "expert", [(i, i ^ j) for i in range(count)]))
    return jnp.concatenate(got, axis=0)


def exchange(rows, experts):
    rows = rows.reshape(experts, CAP, -1)
    rows = lax.all_to_all(rows, "expert", split_axis=0, concat_axis=0, tiled=True)
    return rows.reshape(experts * CAP, -1)


def on_device(tokens, cotangent, expert_ids, route_probs, w_up, w_down):
    experts = lax.axis_size("expert")
    dp_count = lax.axis_size("dp")
    width = tokens.shape[1]
    step = padded(width)
    slot_count = experts * CAP
    ids = expert_ids.T
    probs = route_probs.T
    up_weight = w_up[0]
    down_weight = w_down[0]
    direct = experts > 1 and experts & (experts - 1) == 0
    send, hold = route(
        ids, probs, tokens, cotangent, (up_weight, down_weight), slot_count, direct
    )
    rows = dispatch(send) if direct else exchange(send[0], experts)
    if dp_count > 1 and dp_count & (dp_count - 1) == 0:
        hidden = contract(rows[:, :width], up_weight, 1, 0)
        give, keep = split(hidden)
        give, ahead = lax.optimization_barrier((give, rows))
        query = contract(ahead[:, step : step + width], down_weight, 1, 1)
        hidden_terms = summed(give, keep)
        query_terms = summed(*split(query))
        packed = activate(*hidden_terms, *query_terms)
        back, act, hidden_grad = returned(packed, swap(packed, 1), up_weight, direct)
    else:
        hidden = contract(rows[:, :width], up_weight, 1, 0)
        query = contract(rows[:, step : step + width], down_weight, 1, 1)
        hidden, query = lax.psum((hidden, query), "dp")
        sigma_h = jax.nn.sigmoid(hidden)
        act = (hidden * sigma_h).astype(jnp.bfloat16)
        score = jnp.sum(act.astype(jnp.float32) * query, axis=1, keepdims=True).astype(jnp.bfloat16)
        hidden_grad = (query * sigma_h * (1.0 + hidden * (1.0 - sigma_h))).astype(jnp.bfloat16)
        pad = jnp.zeros((slot_count, step - width), jnp.bfloat16)
        row_grad = contract(hidden_grad, up_weight, 1, 1).astype(jnp.bfloat16)
        back = jnp.concatenate([row_grad, pad, jnp.broadcast_to(score, (slot_count, LANES))], axis=1)
        if direct:
            order = jnp.arange(slot_count, dtype=jnp.int32) ^ (lax.axis_index("expert") * CAP)
            back = back[order]
    back = exchange(back, experts)
    grad_up = contract(rows[:, :width], hidden_grad, 0, 0).astype(jnp.bfloat16)[None]
    grad_down = contract(act, rows[:, step : step + width], 0, 0).astype(jnp.bfloat16)[None]
    grad_tokens, grad_probs = collect(ids, probs, hold, back, width)
    return (grad_tokens, grad_probs.T, grad_up, grad_down)


def solution(mesh):
    in_specs = (
        P("expert", "dp"),
        P("expert", "dp"),
        P("expert", None),
        P("expert", None),
        P("expert", "dp", None),
        P("expert", None, "dp"),
    )
    out_specs = (
        P("expert", "dp"),
        P("expert", None),
        P("expert", "dp", None),
        P("expert", None, "dp"),
    )

    return jax.shard_map(on_device, mesh=mesh, in_specs=in_specs, out_specs=out_specs, check_vma=False)
```

```python
import jax
import jax.numpy as jnp
from jax import lax
from jax.experimental import pallas as pl
from jax.experimental.pallas import tpu as pltpu
from jax.sharding import PartitionSpec as P

CAP = 8
LANES = 128
VMEM = pl.BlockSpec(memory_space=pltpu.VMEM)
ANY = pl.BlockSpec(memory_space=pl.ANY)
HBM = pl.BlockSpec(memory_space=pltpu.HBM)


def contract(left, right, left_dim, right_dim):
    return lax.dot_general(
        left, right, (((left_dim,), (right_dim,)), ((), ())), preferred_element_type=jnp.float32
    )


def swap(value, bit):
    count = lax.axis_size("dp")
    return lax.ppermute(value, "dp", [(i, i ^ bit) for i in range(count)])


def padded(width):
    return -(-width // LANES) * LANES


def chunks(width, wanted):
    return [(at, min(at + wanted, width)) for at in range(0, width, wanted)]


def in_vmem(value):
    return pltpu.with_memory_space_constraint(value, pltpu.VMEM)


def in_hbm(value):
    return pltpu.with_memory_space_constraint(value, pltpu.HBM)


def params(mib):
    return pltpu.CompilerParams(vmem_limit_bytes=mib << 20)


def cost(flops, nbytes):
    return pl.CostEstimate(flops=flops, bytes_accessed=nbytes, transcendentals=0)


def reorder(rows, me):
    count = rows.shape[0]
    here = lax.broadcasted_iota(jnp.int32, (count, count), 0)
    there = lax.broadcasted_iota(jnp.int32, (count, count), 1)
    moves = jnp.where(here == (there ^ (me * CAP)), 1.0, 0.0).astype(jnp.bfloat16)
    return contract(moves, rows, 1, 0).astype(jnp.bfloat16)


def route(ids, probs, tokens, cotangent, weights, slot_count, direct):
    names, block_rows = ids.shape
    width = tokens.shape[1]
    step = padded(width)

    def kernel(ids_hbm, probs_hbm, tok_hbm, cot_hbm, *refs):
        *send_refs, hold_ref, ids_ref, probs_ref, tok, cot, sems = refs[len(weights) :]
        me = lax.axis_index("expert") if direct else 0

        def store(rows, low, high):
            each = slot_count // len(send_refs)
            for j, send_ref in enumerate(send_refs):
                send_ref[:, low:high] = rows[j * each : (j + 1) * each].astype(jnp.bfloat16)

        copies = [
            pltpu.make_async_copy(source, target, sems.at[n])
            for n, (source, target) in enumerate(
                ((ids_hbm, ids_ref), (probs_hbm, probs_ref), (tok_hbm, tok), (cot_hbm, cot))
            )
        ]
        for copy in copies:
            copy.start()
        slots = lax.broadcasted_iota(jnp.int32, (slot_count, block_rows), 0)
        expert = lax.shift_right_logical(slots, CAP.bit_length() - 1) ^ me
        place = (slots & (CAP - 1)).astype(jnp.float32)
        before = lax.broadcasted_iota(jnp.int32, (block_rows, block_rows), 0)
        after = lax.broadcasted_iota(jnp.int32, (block_rows, block_rows), 1)
        earlier = jnp.where(before < after, 1.0, 0.0).astype(jnp.bfloat16)
        member = jnp.zeros((slot_count, block_rows), jnp.float32)
        gate = jnp.zeros((slot_count, block_rows), jnp.float32)
        copies[0].wait()
        copies[1].wait()
        for k in range(names):
            named = ids_ref[k : k + 1, :] == expert
            member = jnp.where(named, 1.0, member)
            gate = jnp.where(named, probs_ref[k : k + 1, :].astype(jnp.float32), gate)
        rank = contract(member.astype(jnp.bfloat16), earlier, 1, 0)
        held = jnp.where(rank == place, member, 0.0)
        gates = jnp.sum(held * gate, axis=1, keepdims=True)
        hold = held.astype(jnp.bfloat16)
        hold_ref[...] = reorder(hold, me) if direct else hold
        copies[2].wait()
        for low, high in chunks(width, 256):
            store(contract(hold, tok[:, low:high], 1, 0), low, high)
        copies[3].wait()
        for low, high in chunks(width, 256):
            store(contract(hold, cot[:, low:high], 1, 0) * gates, step + low, step + high)

    pieces = slot_count // CAP if direct else 1
    *send, hold = pl.pallas_call(
        kernel,
        out_shape=(pltpu.VMEM((slot_count // pieces, 2 * step), jnp.bfloat16),) * pieces
        + (pltpu.VMEM((slot_count, block_rows), jnp.bfloat16),),
        in_specs=[HBM] * (4 + len(weights)),
        out_specs=(VMEM,) * (pieces + 1),
        scratch_shapes=[
            pltpu.VMEM(ids.shape, ids.dtype),
            pltpu.VMEM(probs.shape, probs.dtype),
            pltpu.VMEM(tokens.shape, jnp.bfloat16),
            pltpu.VMEM(tokens.shape, jnp.bfloat16),
            pltpu.SemaphoreType.DMA((4,)),
        ],
        compiler_params=params(8),
        cost_estimate=cost(4 * slot_count * block_rows * width, 8 * block_rows * width),
        name="route",
    )(*map(in_hbm, (ids, probs, tokens, cotangent, *weights)))
    return send, hold


def turned(weight):
    rows, columns = weight.shape

    def kernel(weight_ref, out_ref):
        for low, high in chunks(rows, 256):
            out_ref[:, low:high] = weight_ref[low:high, :].T

    return pl.pallas_call(
        kernel,
        out_shape=pltpu.VMEM((columns, rows), weight.dtype),
        in_specs=[VMEM],
        out_specs=VMEM,
        compiler_params=params(8),
        cost_estimate=cost(0, 4 * weight.size),
        name="turned",
    )(in_vmem(weight))


def core_rows(half):
    core = lax.axis_index("dp") & 1
    return pl.multiple_of(core * half, half), pl.multiple_of((1 - core) * half, half)


def split(value):
    rows, units = value.shape
    half = rows // 2

    def kernel(value_ref, give_ref, keep_ref):
        mine, other = core_rows(half)
        give_ref[...] = value_ref[pl.ds(other, half), :].astype(jnp.bfloat16)
        keep_ref[...] = value_ref[pl.ds(mine, half), :]

    return pl.pallas_call(
        kernel,
        out_shape=(
            jax.ShapeDtypeStruct((half, units), jnp.bfloat16),
            jax.ShapeDtypeStruct((half, units), jnp.float32),
        ),
        in_specs=[VMEM],
        out_specs=(VMEM, VMEM),
        compiler_params=params(8),
        cost_estimate=cost(0, 10 * half * units),
        name="split",
    )(value)


def summed(give, keep):
    own = (keep + swap(give, 1).astype(jnp.float32)).astype(jnp.bfloat16)
    other = jnp.zeros_like(own)
    bit = 2
    while bit < lax.axis_size("dp"):
        if bit > 2:
            own = (own.astype(jnp.float32) + other.astype(jnp.float32)).astype(jnp.bfloat16)
        other = swap(own, bit)
        bit *= 2
    return own, other


def activate(*terms):
    half, units = terms[0].shape

    def kernel(hidden_own, hidden_other, query_own, query_other, out_ref):
        hidden = hidden_own[...].astype(jnp.float32) + hidden_other[...].astype(jnp.float32)
        query = query_own[...].astype(jnp.float32) + query_other[...].astype(jnp.float32)
        sigma_h = jax.nn.sigmoid(hidden)
        act = (hidden * sigma_h).astype(jnp.bfloat16)
        score = jnp.sum(act.astype(jnp.float32) * query, axis=1, keepdims=True)
        grad = query * sigma_h * (1.0 + hidden * (1.0 - sigma_h))
        out_ref[:, :units] = act
        out_ref[:, units : 2 * units] = grad.astype(jnp.bfloat16)
        out_ref[:, 2 * units :] = jnp.broadcast_to(score, (half, LANES)).astype(jnp.bfloat16)

    return pl.pallas_call(
        kernel,
        out_shape=jax.ShapeDtypeStruct((half, 2 * units + LANES), jnp.bfloat16),
        in_specs=[VMEM] * 4,
        out_specs=VMEM,
        compiler_params=params(16),
        cost_estimate=cost(20 * half * units, 12 * half * units),
        name="activate",
    )(*terms)


def returned(own, other, up_turned, direct):
    half = own.shape[0]
    units, width = up_turned.shape
    step = padded(width)

    def kernel(own_ref, other_ref, up_ref, send_ref, act_ref, grad_ref):
        for at, source in zip(core_rows(half), (own_ref, other_ref)):
            act_ref[pl.ds(at, half), :] = source[:, :units]
            grad_ref[pl.ds(at, half), :] = source[:, units : 2 * units]
            send_ref[pl.ds(at, half), step:] = source[:, 2 * units :]
        grad = grad_ref[...]
        if direct:
            me = lax.axis_index("expert")
            grad = reorder(grad, me)
            send_ref[:, step:] = reorder(send_ref[:, step:], me)
        for low, high in chunks(width, 256):
            send_ref[:, low:high] = contract(grad, up_ref[:, low:high], 1, 0).astype(
                jnp.bfloat16
            )

    return pl.pallas_call(
        kernel,
        out_shape=(
            pltpu.VMEM((2 * half, step + LANES), jnp.bfloat16),
            pltpu.VMEM((2 * half, units), jnp.bfloat16),
            pltpu.VMEM((2 * half, units), jnp.bfloat16),
        ),
        in_specs=[VMEM, VMEM, VMEM],
        out_specs=(VMEM, VMEM, VMEM),
        compiler_params=params(8),
        cost_estimate=cost(4 * half * width * units, 2 * width * units),
        name="returned",
    )(own, other, in_vmem(up_turned))


def collect(ids, probs, hold, back, width):
    names, block_rows = ids.shape
    slot_count = hold.shape[0]
    experts = slot_count // CAP
    step = padded(width)
    parts = chunks(width, 256)

    def kernel(ids_ref, probs_ref, hold_ref, back_ref, tok_ref, prob_ref, buf, sems):
        pushes = []
        for n, (low, high) in enumerate(parts):
            buf[:, low:high] = contract(hold_ref[...], back_ref[:, low:high], 0, 0).astype(jnp.bfloat16)
            push = pltpu.make_async_copy(buf.at[:, low:high], tok_ref.at[:, low:high], sems.at[n])
            push.start()
            pushes.append(push)
        scores = hold_ref[...].astype(jnp.float32) * back_ref[:, step : step + 1].astype(jnp.float32)
        total = jnp.zeros((names, block_rows), jnp.float32)
        for e in range(experts):
            score = jnp.sum(scores[e * CAP : (e + 1) * CAP, :], axis=0, keepdims=True)
            total = jnp.where(ids_ref[...] == e, score, total)
        prob_ref[...] = (total / probs_ref[...].astype(jnp.float32)).astype(jnp.bfloat16)
        for push in pushes:
            push.wait()

    return pl.pallas_call(
        kernel,
        out_shape=(
            jax.ShapeDtypeStruct((block_rows, width), jnp.bfloat16),
            jax.ShapeDtypeStruct((names, block_rows), jnp.bfloat16),
        ),
        in_specs=[VMEM] * 4,
        out_specs=(ANY, VMEM),
        scratch_shapes=[
            pltpu.VMEM((block_rows, width), jnp.bfloat16),
            pltpu.SemaphoreType.DMA((len(parts),)),
        ],
        compiler_params=params(16),
        cost_estimate=cost(2 * slot_count * block_rows * width, 4 * block_rows * width),
        name="collect",
    )(ids, probs, hold, back)


def direct_size(experts):
    return experts > 1 and experts & (experts - 1) == 0


def dispatch(pieces):
    count = len(pieces)
    got = [pieces[0]]
    for j in range(1, count):
        got.append(lax.ppermute(pieces[j], "expert", [(i, i ^ j) for i in range(count)]))
    return jnp.concatenate(got, axis=0)


def exchange(rows, experts):
    rows = rows.reshape(experts, CAP, -1)
    rows = lax.all_to_all(rows, "expert", split_axis=0, concat_axis=0, tiled=True)
    return rows.reshape(experts * CAP, -1)


def on_device(tokens, cotangent, expert_ids, route_probs, w_up, w_down):
    experts = lax.axis_size("expert")
    dp_count = lax.axis_size("dp")
    width = tokens.shape[1]
    step = padded(width)
    slot_count = experts * CAP
    ids = expert_ids.T
    probs = route_probs.T
    up_weight = w_up[0]
    down_weight = w_down[0]
    direct = direct_size(experts)
    send, hold = route(
        ids, probs, tokens, cotangent, (up_weight, down_weight), slot_count, direct
    )
    rows = dispatch(send) if direct else exchange(send[0], experts)
    if dp_count > 1 and dp_count & (dp_count - 1) == 0:
        up_turned, down_turned = turned(up_weight), turned(down_weight)
        hidden = contract(rows[:, :width], up_weight, 1, 0)
        give, keep = split(hidden)
        give, ahead = lax.optimization_barrier((give, rows))
        query = contract(ahead[:, step : step + width], down_turned, 1, 0)
        hidden_terms = summed(give, keep)
        query_terms = summed(*split(query))
        packed = activate(*hidden_terms, *query_terms)
        back, act, hidden_grad = returned(packed, swap(packed, 1), up_turned, direct)
    else:
        hidden = contract(rows[:, :width], up_weight, 1, 0)
        query = contract(rows[:, step : step + width], down_weight, 1, 1)
        hidden, query = lax.psum((hidden, query), "dp")
        sigma_h = jax.nn.sigmoid(hidden)
        act = (hidden * sigma_h).astype(jnp.bfloat16)
        score = jnp.sum(act.astype(jnp.float32) * query, axis=1, keepdims=True).astype(jnp.bfloat16)
        hidden_grad = (query * sigma_h * (1.0 + hidden * (1.0 - sigma_h))).astype(jnp.bfloat16)
        pad = jnp.zeros((slot_count, step - width), jnp.bfloat16)
        row_grad = contract(hidden_grad, up_weight, 1, 1).astype(jnp.bfloat16)
        back = jnp.concatenate([row_grad, pad, jnp.broadcast_to(score, (slot_count, LANES))], axis=1)
        if direct:
            order = jnp.arange(slot_count, dtype=jnp.int32) ^ (lax.axis_index("expert") * CAP)
            back = back[order]
    back = exchange(back, experts)
    grad_up = contract(rows[:, :width], hidden_grad, 0, 0).astype(jnp.bfloat16)[None]
    grad_down = contract(act, rows[:, step : step + width], 0, 0).astype(jnp.bfloat16)[None]
    grad_tokens, grad_probs = collect(ids, probs, hold, back, width)
    return (grad_tokens, grad_probs.T, grad_up, grad_down)


def solution(mesh):
    in_specs = (
        P("expert", "dp"),
        P("expert", "dp"),
        P("expert", None),
        P("expert", None),
        P("expert", "dp", None),
        P("expert", None, "dp"),
    )
    out_specs = (
        P("expert", "dp"),
        P("expert", None),
        P("expert", "dp", None),
        P("expert", None, "dp"),
    )

    return jax.shard_map(on_device, mesh=mesh, in_specs=in_specs, out_specs=out_specs, check_vma=False)
```
